256 devices in a mesh: span: 8 (over x, y_hi), stream: 32 (over z, y_lo, core).
Axes of the slice: x: 4, y: 4 (y_hi: 2, y_lo: 2; y = y_hi * 2 + y_lo), z: 8, core: 2. Of those that a mesh axis runs over, the one named last changes fastest.
Arguments:
- state: float32 [6, 64, 131072], P(None, None, ('span', 'stream')), may hold values from -6 to 6
- stiffness: float32 [131072], P(('span', 'stream')), may hold values from 0.3 to 6
- crossing: int32 [2, 32768], P(None, ('span', 'stream')), may hold values from 0 to 511, as said below
- contact_send: int32 [2, 8, 262144], P(None, None, ('span', 'stream')), may hold values from 0 to 32767
- contact_recv: int32 [2, 8, 262144], P(None, None, ('span', 'stream')), may hold values from 0 to 32767
- contact_fill: int32 [2, 8, 2048], P(None, None, ('span', 'stream')), may hold values from 0 to 128, as said below
Outputs:
- final_state: float32 [6, 64, 131072], P(None, None, ('span', 'stream'))
The draws below stay inside these ranges and needn't reach their ends.
Inputs may be any that keep to these rules, and one draw needn't show every extreme that they name: `crossing`: each slab's 2 * 64 entries of one step are distinct and include slots 0 and 511. `contact_fill`: in each run of 8 blocks the live blocks come first; all full except the last live one; some runs have every block live.
All inputs are finite; a program needn't handle non-finite values.
Results may differ from the reference program's by a relative error of at most 0.0001.
Values sent between devices are 32-bit elements; how exact they have to be, the bound alone decides.
No kernel may reach another device: no remote copies, remote signals or barrier semaphores. Data moves between devices by JAX's collectives and lax.ppermute only.
A program may use at most 128 MiB of HBM per device.

```python
import math
import jax
import jax.numpy as jnp
from jax import lax

NODES = 64
FIELDS = 6
STEPS = 2
F_DEV = 512
M = 64
CB = 8
FIBRES = 131072
N_SPAN = 8
N_STREAM = 32


def draw_crossing(key, part):
    ndev = N_SPAN * N_STREAM
    keys = jax.random.split(key, STEPS * ndev)

    def single(subkey):
        inner = jax.random.permutation(subkey, F_DEV - 2) + 1
        listed = jnp.concatenate([jnp.array([0, F_DEV - 1], dtype=jnp.int32), inner[:2 * M - 2].astype(jnp.int32)])
        return jax.random.permutation(jax.random.fold_in(subkey, 7), listed)
    return jax.vmap(single)(keys).reshape(STEPS, ndev * 2 * M).astype(jnp.int32)


def draw_contact_fill(key, part):
    ndev = N_SPAN * N_STREAM
    shape = (STEPS, N_SPAN, ndev)
    livecount = jax.random.randint(jax.random.fold_in(key, 11), shape, 0, CB + 1)
    flat_pos = jnp.arange(STEPS * N_SPAN * ndev, dtype=jnp.int32).reshape(shape)
    livecount = jnp.where(flat_pos == 0, CB, livecount)
    lastfill = jax.random.randint(jax.random.fold_in(key, 12), shape, 1, 129)
    block = jnp.arange(CB, dtype=jnp.int32)
    full = block[None, None, None, :] < livecount[..., None] - 1
    last = block[None, None, None, :] == livecount[..., None] - 1
    fill = jnp.where(full, 128, jnp.where(last, lastfill[..., None], 0))
    return fill.reshape(STEPS, N_SPAN, ndev * CB).astype(jnp.int32)


def plant(drawn, rng, least, top_value):
    longest = drawn.shape.index(max(drawn.shape))
    spots = []
    for shift in (0, 1):
        where = [jax.random.randint(jax.random.fold_in(rng, axis), (), 0, length) for axis, length in enumerate(drawn.shape)]
        where[longest] = (where[longest] + shift) % drawn.shape[longest]
        spots.append(tuple(where))
    return drawn.at[spots[0]].set(least).at[spots[1]].set(top_value)


def block_levels(stream_key, dims, shards, low, top_value):
    gain, own = 1.0, jax.random.fold_in(stream_key, 6)
    for axis_at, blocks in shards:
        heights = jnp.exp(jax.random.uniform(jax.random.fold_in(own, axis_at), (blocks,), jnp.float32, low / len(shards), top_value / len(shards)))
        gain = gain * jnp.repeat(heights, dims[axis_at] // blocks).reshape([-1 if axis == axis_at else 1 for axis in range(len(dims))])
    return gain


def centred(stream_key, dims, spread, bound, cuts=(), held_as=jnp.bfloat16):
    values = spread * jax.random.normal(stream_key, dims, jnp.float32)
    if cuts:
        values = values * block_levels(stream_key, dims, cuts, -0.22, 0.18)
    return jnp.clip(values, -bound, bound).astype(held_as)


def setup_inputs(seed: int = 0) -> dict:
    streams_of = jax.random.split(jax.random.key(seed), 7)
    state = centred(streams_of[0], (FIELDS, NODES, FIBRES), 1.0, 6.0, ((2, 256),), jnp.float32)
    stiffness = jnp.clip(jnp.exp(math.log(6.0) - 2.9957322 * jax.random.uniform(streams_of[1], (FIBRES,), jnp.float32) ** block_levels(streams_of[1], (FIBRES,), ((0, 256),), -0.2, 0.2)), 0.3, 6.0)
    crossing = draw_crossing(jax.random.fold_in(streams_of[6], 71), 0)
    contact_send = plant(jax.random.randint(streams_of[3], (STEPS, N_SPAN, CB * 128 * N_SPAN * N_STREAM), 0, NODES * F_DEV), jax.random.fold_in(streams_of[3], 1), 0, (NODES * F_DEV) - 1).astype(jnp.int32)
    contact_recv = plant(jax.random.randint(streams_of[4], (STEPS, N_SPAN, CB * 128 * N_SPAN * N_STREAM), 0, NODES * F_DEV), jax.random.fold_in(streams_of[4], 1), 0, (NODES * F_DEV) - 1).astype(jnp.int32)
    contact_fill = draw_contact_fill(jax.random.fold_in(streams_of[6], 71), 0)
    return dict(state=state, stiffness=stiffness, crossing=crossing, contact_send=contact_send, contact_recv=contact_recv, contact_fill=contact_fill)


def thomas(coef, rhs):
    count = rhs.shape[1]
    first = 1.0 + coef
    cps = [-coef / first]
    ds = [rhs[:, 0] / first]
    for node in range(1, count):
        diag = 1.0 + coef if node == count - 1 else 1.0 + 2.0 * coef
        denom = diag + coef * cps[-1]
        cps.append(-coef / denom)
        ds.append((rhs[:, node] + coef * ds[-1]) / denom)
    outs = [ds[-1]]
    for node in range(count - 2, -1, -1):
        outs.append(ds[node] - cps[node] * outs[-1])
    return jnp.stack(outs[::-1], axis=1)


def take_cols(flat, index):
    return flat[:, index]


def reference(state, stiffness, crossing, contact_send, contact_recv, contact_fill):
    ndev = N_SPAN * N_STREAM
    fdev = state.shape[2] // ndev
    nodes = state.shape[1]
    fields = state.shape[0]
    quota = contact_send.shape[2] // ndev
    blocks = quota // 128
    half = crossing.shape[1] // ndev // 2
    xcur = state.reshape(fields, nodes, ndev, fdev).transpose(2, 0, 1, 3)
    coef = stiffness.reshape(ndev, fdev)
    for step in range(STEPS):
        pflat = xcur[:, :3].reshape(ndev, 3, nodes * fdev)
        sidx = contact_send[step].reshape(N_SPAN, ndev, quota).transpose(1, 0, 2)
        sent = jax.vmap(take_cols)(pflat, sidx)
        sent = sent.reshape(N_SPAN, N_STREAM, 3, N_SPAN, quota).transpose(3, 1, 0, 2, 4).reshape(ndev, N_SPAN, 3, quota)
        fill = contact_fill[step].reshape(N_SPAN, ndev, blocks).transpose(1, 0, 2)
        fill = fill.reshape(N_SPAN, N_STREAM, N_SPAN, blocks).transpose(2, 1, 0, 3).reshape(ndev, N_SPAN, blocks)
        live = (jnp.arange(128, dtype=jnp.int32)[None, None, None, :] < fill[..., None]).reshape(ndev, N_SPAN, quota)
        ridx = contact_recv[step].reshape(N_SPAN, ndev, quota).transpose(1, 0, 2)
        local = jax.vmap(take_cols)(pflat, ridx).transpose(0, 2, 1, 3)
        delta = sent - local
        radius = jnp.sum(delta * delta, axis=2, keepdims=True)
        force = jnp.where(live[:, :, None, :], 1.0 * delta / (1.0 + radius), 0.0)

        def gather_force(index, value):
            zero = jnp.zeros((3, nodes * fdev), value.dtype)
            return zero.at[:, index.reshape(-1)].add(value.transpose(1, 0, 2).reshape(3, -1))

        contact = jax.vmap(gather_force)(ridx, force).reshape(ndev, 3, nodes, fdev)
        rhs = jnp.concatenate([xcur[:, :3] + 0.5 * contact, xcur[:, 3:]], axis=1)
        solved = lax.map(lambda pair: thomas(pair[1], pair[0]), (rhs, coef))
        cross = crossing[step].reshape(ndev, 2 * half)
        slots_up = cross[:, :half]
        slots_down = cross[:, half:]
        pick = jax.vmap(lambda u, a: u[:, :, a])
        pick_c = jax.vmap(lambda u, a: u[a])
        shape5 = (N_SPAN, N_STREAM, fields, nodes, half)
        arrive_up = jnp.roll(pick(solved, slots_up).reshape(shape5), 1, axis=1).reshape(ndev, fields, nodes, half)
        arrive_down = jnp.roll(pick(solved, slots_down).reshape(shape5), -1, axis=1).reshape(ndev, fields, nodes, half)
        coef_up = jnp.roll(pick_c(coef, slots_up).reshape(N_SPAN, N_STREAM, half), 1, axis=1).reshape(ndev, half)
        coef_down = jnp.roll(pick_c(coef, slots_down).reshape(N_SPAN, N_STREAM, half), -1, axis=1).reshape(ndev, half)
        xcur = jax.vmap(lambda u, a, b, p, q: u.at[:, :, a].set(p).at[:, :, b].set(q))(solved, slots_up, slots_down, arrive_up, arrive_down)
        coef = jax.vmap(lambda u, a, b, p, q: u.at[a].set(p).at[b].set(q))(coef, slots_up, slots_down, coef_up, coef_down)
    return xcur.transpose(1, 2, 0, 3).reshape(fields, nodes, ndev * fdev)
```

```python
import functools

import jax
import jax.numpy as jnp
from jax import lax
from jax.experimental import pallas as pl
from jax.experimental.pallas import tpu as pltpu
from jax.sharding import PartitionSpec as P

STEPS = 2
BLOCK = 128
F32 = jnp.float32
BF16 = jnp.bfloat16
VMEM_LIMIT = 48 * 1024 * 1024


def split2(x):
    hi = x.astype(BF16)
    lo = (x - hi.astype(F32)).astype(BF16)
    return hi, lo


def split3(x):
    hi = x.astype(BF16)
    rest = x - hi.astype(F32)
    mid = rest.astype(BF16)
    lo = (rest - mid.astype(F32)).astype(BF16)
    return hi, mid, lo


def hot(index, count):
    rows = lax.broadcasted_iota(jnp.int32, (count, index.shape[1]), 0)
    return jnp.where(rows == index, 1.0, 0.0).astype(BF16)


def dot_nt(a, b):
    return lax.dot_general(a, b, (((1,), (1,)), ((), ())), preferred_element_type=F32)


def gather_row(table, index, nodes, fdev):
    slot = jnp.bitwise_and(index, fdev - 1)
    node = jnp.right_shift(index, fdev.bit_length() - 1)
    got = jnp.dot(table, hot(slot, fdev), preferred_element_type=F32)
    half = 3 * nodes
    got = got[:half] + got[half:]
    mask = lax.broadcasted_iota(jnp.int32, (nodes, index.shape[1]), 0) == node
    return [
        jnp.sum(jnp.where(mask, got[c * nodes : (c + 1) * nodes], 0.0), axis=0, keepdims=True)
        for c in range(3)
    ]


def store_table(table_ref, positions):
    hi, lo = split2(positions)
    half = positions.shape[0]
    table_ref[:half] = hi
    table_ref[half:] = lo


def send_gather(table_ref, index_ref, fill_ref, out_ref, nodes, fdev):
    groups, quota = index_ref.shape
    lane = lax.broadcasted_iota(jnp.int32, (1, BLOCK), 1)

    @pl.loop(0, groups)
    def _(g):
        rows = gather_row(table_ref[...], index_ref[pl.ds(g, 1), :], nodes, fdev)
        for c in range(3):
            out_ref[g, pl.ds(c, 1), :] = rows[c]
        for b in range(quota // BLOCK):
            live = jnp.where(lane < fill_ref[g, b], 1.0, 0.0)
            out_ref[g, pl.ds(3, 1), pl.ds(b * BLOCK, BLOCK)] = live


def fold(values, rows_ref):
    rows = values.shape[0]
    for i in range(values.shape[1] // BLOCK):
        rows_ref[i * rows : (i + 1) * rows] = values[:, i * BLOCK : (i + 1) * BLOCK]


def unfold(rows_ref, rows):
    chunks = rows_ref.shape[0] // rows
    return jnp.concatenate([rows_ref[i * rows : (i + 1) * rows] for i in range(chunks)], axis=1)


def fold_coef(coef, fields):
    chunks = coef.shape[1] // BLOCK
    return jnp.concatenate(
        [jnp.broadcast_to(coef[:, i * BLOCK : (i + 1) * BLOCK], (fields, BLOCK)) for i in range(chunks)], axis=0
    )


def factor(coef, inv_ref, elim_ref):
    inv = 1.0 / (1.0 + coef)
    for k in range(inv_ref.shape[0]):
        if k:
            inv = 1.0 / (1.0 + 2.0 * coef - coef * elim)
        elim = coef * inv
        inv_ref[k] = inv
        elim_ref[k] = elim


def solve(rows_ref, coef, inv_ref, elim_ref, nodes):
    half = nodes // 2
    lines = coef.shape[0]

    def at(n):
        return rows_ref[pl.ds(n, lines, stride=nodes), :]

    def put(n, value):
        rows_ref[pl.ds(n, lines, stride=nodes), :] = value

    top = at(0) * inv_ref[0]
    bot = at(nodes - 1) * inv_ref[0]
    tops, bots = [top], [bot]
    for k in range(1, half - 1):
        inv = inv_ref[k]
        elim = elim_ref[k]
        top = at(k) * inv + elim * top
        bot = at(nodes - 1 - k) * inv + elim * bot
        tops.append(top)
        bots.append(bot)
    left = at(half - 1) + coef * top
    right = at(half) + coef * bot
    pivot = 1.0 + 2.0 * coef - coef * elim_ref[half - 2]
    even = (left + right) * (0.5 / (pivot - coef))
    odd = (left - right) * (0.5 / (pivot + coef))
    top, bot = even + odd, even - odd
    put(half - 1, top)
    put(half, bot)
    for k in range(half - 2, -1, -1):
        elim = elim_ref[k]
        top = tops[k] + elim * top
        bot = bots[k] + elim * bot
        put(k, top)
        put(nodes - 1 - k, bot)


def pick(values, cross_hot):
    rows = values.shape[0]
    got = jnp.dot(jnp.concatenate(split3(values), axis=0), cross_hot, preferred_element_type=F32)
    return (got[:rows] + got[rows : 2 * rows]) + got[2 * rows :]


def place(values, cross_hot):
    rows = values.shape[0]
    got = dot_nt(jnp.concatenate(split3(values), axis=0), cross_hot)
    return (got[:rows] + got[rows : 2 * rows]) + got[2 * rows :]


def pack(leavers):
    rows = leavers.shape[0] // 2
    half = leavers.shape[1] // 2
    first, second = leavers[:rows], leavers[rows:]
    low = lax.broadcasted_iota(jnp.int32, first.shape, 1) < half
    up = jnp.where(low, first, pltpu.roll(second, half, 1))
    down = jnp.where(low, pltpu.roll(first, half, 1), second)
    return up, down


def unpack(up, down):
    half = up.shape[1] // 2
    low = lax.broadcasted_iota(jnp.int32, up.shape, 1) < half
    first = jnp.where(low, up, pltpu.roll(down, half, 1))
    second = jnp.where(low, pltpu.roll(up, half, 1), down)
    return first, second


def first_kernel(state_ref, index_ref, fill_ref, out_ref, table_ref, *, nodes, fdev):
    store_table(table_ref, state_ref[: 3 * nodes])
    send_gather(table_ref, index_ref, fill_ref, out_ref, nodes, fdev)


def local_kernel(
    state_ref, coef_ref, cross_ref, index_ref,
    local_ref, inv_ref, elim_ref, rot_ref, up_ref, down_ref,
    table_ref, rows_ref, *, nodes, fdev,
):
    half_rows = 3 * nodes
    groups = index_ref.shape[0]
    store_table(table_ref, state_ref[:half_rows])

    @pl.loop(0, groups)
    def _(g):
        rows = gather_row(table_ref[...], index_ref[pl.ds(g, 1), :], nodes, fdev)
        for c in range(3):
            local_ref[g, pl.ds(c, 1), :] = rows[c]

    coef = coef_ref[...]
    folded = fold_coef(coef, 3)
    factor(folded, inv_ref, elim_ref)
    fold(state_ref[half_rows:], rows_ref)
    solve(rows_ref, folded, inv_ref, elim_ref, nodes)
    rot_ref[...] = unfold(rows_ref, half_rows)
    cross_hot = hot(cross_ref[...], fdev)
    up, down = pack(pick(rot_ref[...], cross_hot))
    rows = up.shape[0]
    up_ref[:rows] = up
    down_ref[:rows] = down
    moved = pick(jnp.broadcast_to(coef, (8, fdev)), cross_hot)
    up_ref[rows:] = moved
    down_ref[rows:] = pltpu.roll(moved, moved.shape[1] // 2, 1)


def contact_kernel(
    got_ref, local_ref, index_ref, state_ref, coef_ref, inv_ref, elim_ref, cross_ref, rup_ref, rdown_ref,
    pos_ref, up_ref, down_ref,
    acc_ref, rows_ref, *, nodes, fdev,
):
    half_rows = 3 * nodes
    groups = index_ref.shape[0]
    acc_ref[...] = jnp.zeros_like(acc_ref)

    @pl.loop(0, groups)
    def _(g):
        index = index_ref[pl.ds(g, 1), :]
        slot = jnp.bitwise_and(index, fdev - 1)
        node = jnp.right_shift(index, fdev.bit_length() - 1)
        delta = [got_ref[g, pl.ds(c, 1), :] - local_ref[g, pl.ds(c, 1), :] for c in range(3)]
        radius = delta[0] * delta[0] + delta[1] * delta[1] + delta[2] * delta[2]
        scale = jnp.where(got_ref[g, pl.ds(3, 1), :] > 0.5, 1.0 / (1.0 + radius), 0.0)
        mask = lax.broadcasted_iota(jnp.int32, (nodes, index.shape[1]), 0) == node
        highs, lows = [], []
        for c in range(3):
            hi, lo = split2(delta[c] * scale)
            highs.append(jnp.where(mask, hi.astype(F32), 0.0).astype(BF16))
            lows.append(jnp.where(mask, lo.astype(F32), 0.0).astype(BF16))
        spread = jnp.concatenate(highs + lows, axis=0)
        acc_ref[...] += dot_nt(spread, hot(slot, fdev))

    fold(state_ref[:half_rows] + 0.5 * (acc_ref[:half_rows] + acc_ref[half_rows:]), rows_ref)
    solve(rows_ref, fold_coef(coef_ref[...], 3), inv_ref, elim_ref, nodes)
    pos_ref[...] = unfold(rows_ref, half_rows)
    up, down = pack(pick(pos_ref[...], hot(cross_ref[...], fdev)))
    rows = up.shape[0]
    up_ref[:rows] = up
    down_ref[:rows] = down
    up_ref[rows:] = rup_ref[...]
    down_ref[rows:] = rdown_ref[...]


def arrive(up_ref, down_ref, pos_ref, rot_ref, cross_ref, out_ref, nodes, fdev):
    part = 3 * nodes // 2
    cross_hot = hot(cross_ref[...], fdev)
    ones = jnp.ones((8, cross_hot.shape[1]), BF16)
    keep = dot_nt(ones, cross_hot)[0:1] < 0.5
    for side, ref in ((0, pos_ref), (1, rot_ref)):
        rows = pl.ds(side * part, part)
        first, second = unpack(up_ref[rows, :], down_ref[rows, :])
        placed = place(jnp.concatenate([first, second], axis=0), cross_hot)
        out_ref[pl.ds(side * 2 * part, 2 * part), :] = jnp.where(keep, ref[...], placed)
    return cross_hot, keep


def next_kernel(
    up_ref, down_ref, pos_ref, rot_ref, coef_ref, cross_ref, index_ref, fill_ref,
    state_ref, coef_out_ref, out_ref,
    table_ref, *, nodes, fdev,
):
    cross_hot, keep = arrive(up_ref, down_ref, pos_ref, rot_ref, cross_ref, state_ref, nodes, fdev)
    rows = pl.ds(3 * nodes, 8)
    first, _ = unpack(up_ref[rows, :], down_ref[rows, :])
    coef_out_ref[...] = jnp.where(keep, coef_ref[...], place(first, cross_hot)[0:1])
    store_table(table_ref, state_ref[: 3 * nodes])
    send_gather(table_ref, index_ref, fill_ref, out_ref, nodes, fdev)


def last_kernel(up_ref, down_ref, pos_ref, rot_ref, cross_ref, state_ref, *, nodes, fdev):
    arrive(up_ref, down_ref, pos_ref, rot_ref, cross_ref, state_ref, nodes, fdev)


def shifted(block, axis, distance):
    devices = range(lax.axis_size(axis))
    route = [((i - distance) % len(devices), i) for i in devices]
    return lax.ppermute(block, axis, route)


def per_device(state, stiffness, crossing, contact_send, contact_recv, contact_fill):
    fields, nodes, fdev = state.shape
    _, groups, quota = contact_send.shape
    cross = crossing.shape[1]
    rows = 3 * nodes
    moved = rows + 8
    vmem = pl.BlockSpec(memory_space=pltpu.VMEM)
    smem = pl.BlockSpec(memory_space=pltpu.SMEM)
    sent_shape = jax.ShapeDtypeStruct((groups, 4, quota), F32)
    table = pltpu.VMEM((2 * rows, fdev), BF16)

    def sds(*shape):
        return jax.ShapeDtypeStruct(shape, F32)

    lines = 3 * fdev // BLOCK
    factors = sds(nodes // 2, lines, BLOCK)
    folded = pltpu.VMEM((lines * nodes, BLOCK), F32)

    def call(kernel, name, ins, outs, scratch, flops):
        return pl.pallas_call(
            functools.partial(kernel, nodes=nodes, fdev=fdev),
            out_shape=outs,
            in_specs=ins,
            out_specs=[vmem] * len(outs),
            scratch_shapes=scratch,
            name=name,
            cost_estimate=pl.CostEstimate(flops=flops, bytes_accessed=4 * fields * nodes * fdev, transcendentals=0),
            compiler_params=pltpu.CompilerParams(vmem_limit_bytes=VMEM_LIMIT),
        )

    matmul = 2 * 2 * rows * fdev * groups * quota
    xcur = state.reshape(fields * nodes, fdev)
    coef = stiffness.reshape(1, fdev)
    (sent,) = call(first_kernel, "send_first", [vmem, vmem, smem], [sent_shape], [table], matmul)(
        xcur, contact_send[0], contact_fill[0]
    )
    for step in range(STEPS):
        got = lax.all_to_all(sent, "span", split_axis=0, concat_axis=0, tiled=True)
        crossing_now = crossing[step].reshape(1, cross)
        local, inv, elim, rot, rup, rdown = call(
            local_kernel, "local", [vmem] * 4,
            [sds(groups, 3, quota), factors, factors, sds(rows, fdev),
             sds(rows // 2 + 8, cross), sds(rows // 2 + 8, cross)],
            [table, folded], matmul,
        )(xcur, coef, crossing_now, contact_recv[step])
        pos, up, down = call(
            contact_kernel, "contact", [vmem] * 10,
            [sds(rows, fdev), sds(moved, cross), sds(moved, cross)],
            [pltpu.VMEM((2 * rows, fdev), F32), folded], matmul,
        )(got, local, contact_recv[step], xcur, coef, inv, elim, crossing_now, rup, rdown)
        up = shifted(up, "stream", 1)
        down = shifted(down, "stream", -1)
        if step + 1 < STEPS:
            xcur, coef, sent = call(
                next_kernel, "send_next", [vmem] * 7 + [smem],
                [sds(fields * nodes, fdev), sds(1, fdev), sent_shape], [table], matmul,
            )(up, down, pos, rot, coef, crossing_now, contact_send[step + 1], contact_fill[step + 1])
        else:
            (xcur,) = call(last_kernel, "arrive", [vmem] * 5, [sds(fields * nodes, fdev)], [], matmul // 8)(
                up, down, pos, rot, crossing_now
            )
    return xcur.reshape(fields, nodes, fdev)


def solution(mesh):
    placed = (
        P(None, None, ("span", "stream")),
        P(("span", "stream")),
        P(None, ("span", "stream")),
        P(None, None, ("span", "stream")),
        P(None, None, ("span", "stream")),
        P(None, None, ("span", "stream")),
    )
    return jax.shard_map(
        per_device,
        mesh=mesh,
        in_specs=placed,
        out_specs=P(None, None, ("span", "stream")),
        check_vma=False,
    )
```

```python
import functools

import jax
import jax.numpy as jnp
from jax import lax
from jax.experimental import pallas as pl
from jax.experimental.pallas import tpu as pltpu
from jax.sharding import PartitionSpec as P

STEPS = 2
BLOCK = 128
LANES = 256
CHUNK = 8
F32 = jnp.float32
BF16 = jnp.bfloat16
VMEM_LIMIT = 48 * 1024 * 1024
FIRST_LIMIT = 63 * 1024 * 1024


def split2(x):
    hi = x.astype(BF16)
    lo = (x - hi.astype(F32)).astype(BF16)
    return hi, lo


def split3(x):
    hi = x.astype(BF16)
    rest = x - hi.astype(F32)
    mid = rest.astype(BF16)
    lo = (rest - mid.astype(F32)).astype(BF16)
    return hi, mid, lo


def hot(index, count):
    rows = lax.broadcasted_iota(jnp.int32, (count, index.shape[1]), 0)
    return jnp.where(rows == index, 1.0, 0.0).astype(BF16)


def dot_nt(a, b):
    return lax.dot_general(a, b, (((1,), (1,)), ((), ())), preferred_element_type=F32)


def parts_of(index, nodes):
    per_node = index >> (LANES.bit_length() - 1)
    lane = index & (LANES - 1)
    return lane, per_node


def row_key(per_node, nodes, fdev):
    wide = fdev // LANES
    return (per_node & (wide - 1)) * nodes + (per_node >> (wide.bit_length() - 1))


def store_table(table_ref, positions, nodes):
    wide = positions.shape[1] // LANES
    rows = 3 * wide * nodes
    for c in range(3):
        for w in range(wide):
            hi, lo = split2(positions[c * nodes : (c + 1) * nodes, w * LANES : (w + 1) * LANES])
            at = (c * wide + w) * nodes
            table_ref[at : at + nodes] = hi
            table_ref[rows + at : rows + at + nodes] = lo


def gather_row(table, index, nodes, fdev, between=lambda: None):
    lane, per_node = parts_of(index, nodes)
    key = row_key(per_node, nodes, fdev)
    got = jnp.dot(table, hot(lane, LANES), preferred_element_type=F32)
    between()
    rows = got.shape[0] // 2
    keys = rows // 3
    relative = key - lax.broadcasted_iota(jnp.int32, (8, index.shape[1]), 0)
    out = []
    for c in range(3):
        acc = jnp.zeros((8, index.shape[1]), F32)
        for j in range(0, keys, 8):
            at = c * keys + j
            acc = jnp.where(relative == j, got[at : at + 8] + got[rows + at : rows + at + 8], acc)
        out.append(jnp.sum(acc, axis=0, keepdims=True))
    return out


def list_live(live_of, list_ref, groups, blocks):
    count = jnp.int32(0)
    for g in range(groups):
        for b in range(blocks):
            list_ref[count] = g * blocks + b
            count = count + live_of(g, b)
    return count


def index_chunk(index_ref, ids, groups, blocks):
    rows = [(n & (blocks - 1)) * groups + (n >> (blocks.bit_length() - 1)) for n in ids]
    return jnp.concatenate([index_ref[pl.ds(n, 1), :] for n in rows], axis=1)


def put_chunk(out_ref, ids, rows, blocks):
    for k, n in enumerate(ids):
        for c in range(3):
            at = c * blocks + (n & (blocks - 1))
            out_ref[n >> (blocks.bit_length() - 1), pl.ds(at, 1), :] = rows[c][:, k * BLOCK : (k + 1) * BLOCK]


def gather_live(table_ref, index_ref, out_ref, list_ref, count, groups, blocks, nodes, fdev):
    @pl.loop(0, (count + CHUNK - 1) // CHUNK)
    def _(i):
        ids = [list_ref[jnp.minimum(i * CHUNK + k, count - 1)] for k in range(CHUNK)]
        index = index_chunk(index_ref, ids, groups, blocks)
        put_chunk(out_ref, ids, gather_row(table_ref[...], index, nodes, fdev), blocks)


def send_gather(table_ref, index_ref, fill_ref, out_ref, list_ref, step, nodes, fdev):
    groups, lines, _ = out_ref.shape
    blocks = lines // 4
    low = lax.broadcasted_iota(jnp.int32, (1, BLOCK), 1) < BLOCK // 2
    out_ref[...] = jnp.zeros_like(out_ref)
    count = list_live(lambda g, b: (fill_ref[step, g, b] > 0).astype(jnp.int32), list_ref, groups, blocks)
    for g in range(groups):
        for b in range(blocks):
            fills = jnp.where(low, fill_ref[step, g, b], fill_ref[STEPS - 1, g, b])
            out_ref[g, pl.ds(3 * blocks + b, 1), :] = fills.astype(F32)
    gather_live(table_ref, index_ref, out_ref, list_ref, count, groups, blocks, nodes, fdev)


def live_words(got_ref, blocks, lane):
    sub = lax.broadcasted_iota(jnp.int32, (blocks, BLOCK), 0)
    here = lax.broadcasted_iota(jnp.int32, (blocks, BLOCK), 1) == lane
    words = []
    for g in range(got_ref.shape[0]):
        live = (got_ref[g, 3 * blocks :] > 0.5) & here
        words.append(jnp.sum(jnp.where(live, jnp.left_shift(1, sub), 0).astype(F32)).astype(jnp.int32))
    return words


def fold(values, rows_ref):
    rows = values.shape[0]
    for i in range(values.shape[1] // BLOCK):
        rows_ref[i * rows : (i + 1) * rows] = values[:, i * BLOCK : (i + 1) * BLOCK]


def unfold(rows_ref, rows):
    chunks = rows_ref.shape[0] // rows
    return jnp.concatenate([rows_ref[i * rows : (i + 1) * rows] for i in range(chunks)], axis=1)


def fold_coef(coef, fields):
    chunks = coef.shape[1] // BLOCK
    return jnp.concatenate(
        [jnp.broadcast_to(coef[:, i * BLOCK : (i + 1) * BLOCK], (fields, BLOCK)) for i in range(chunks)], axis=0
    )


def factor_steps(coef, inv_ref, elim_ref):
    inv = 1.0 / (1.0 + coef)
    for k in range(inv_ref.shape[0]):
        if k:
            inv = 1.0 / (1.0 + 2.0 * coef - coef * elim)
        elim = coef * inv
        inv_ref[k] = inv
        elim_ref[k] = elim
        yield


def solve_steps(get, put, hold_ref, coef, inv_ref, elim_ref, nodes):
    half = nodes // 2
    top = get(0) * inv_ref[0]
    bot = get(nodes - 1) * inv_ref[0]
    hold_ref[0] = top
    hold_ref[nodes - 1] = bot
    for k in range(1, half - 1):
        inv = inv_ref[k]
        elim = elim_ref[k]
        top = get(k) * inv + elim * top
        bot = get(nodes - 1 - k) * inv + elim * bot
        hold_ref[k] = top
        hold_ref[nodes - 1 - k] = bot
        yield
    left = get(half - 1) + coef * top
    right = get(half) + coef * bot
    pivot = 1.0 + 2.0 * coef - coef * elim_ref[half - 2]
    even = (left + right) * (0.5 / (pivot - coef))
    odd = (left - right) * (0.5 / (pivot + coef))
    top, bot = even + odd, even - odd
    put(half - 1, top)
    put(half, bot)
    yield
    for k in range(half - 2, -1, -1):
        elim = elim_ref[k]
        top = hold_ref[k] + elim * top
        bot = hold_ref[nodes - 1 - k] + elim * bot
        put(k, top)
        put(nodes - 1 - k, bot)
        yield


def strided(rows_ref, lines, nodes):
    def get(n):
        return rows_ref[pl.ds(n, lines, stride=nodes), :]

    def put(n, value):
        rows_ref[pl.ds(n, lines, stride=nodes), :] = value

    return get, put


def dense(hold_ref):
    def get(n):
        return hold_ref[n]

    def put(n, value):
        hold_ref[n] = value

    return get, put


def run(steps, count=None):
    done = 0
    while count is None or done < count:
        if next(steps, steps) is steps:
            return
        done += 1


def pick(values, cross_hot):
    rows = values.shape[0]
    got = jnp.dot(jnp.concatenate(split3(values), axis=0), cross_hot, preferred_element_type=F32)
    return (got[:rows] + got[rows : 2 * rows]) + got[2 * rows :]


def place(values, cross_hot):
    rows = values.shape[0]
    got = dot_nt(jnp.concatenate(split3(values), axis=0), cross_hot)
    return (got[:rows] + got[rows : 2 * rows]) + got[2 * rows :]


def pack(leavers):
    rows = leavers.shape[0] // 2
    half = leavers.shape[1] // 2
    first, second = leavers[:rows], leavers[rows:]
    low = lax.broadcasted_iota(jnp.int32, first.shape, 1) < half
    up = jnp.where(low, first, pltpu.roll(second, half, 1))
    down = jnp.where(low, pltpu.roll(first, half, 1), second)
    return up, down


def unpack(up, down):
    half = up.shape[1] // 2
    low = lax.broadcasted_iota(jnp.int32, up.shape, 1) < half
    first = jnp.where(low, up, pltpu.roll(down, half, 1))
    second = jnp.where(low, pltpu.roll(up, half, 1), down)
    return first, second


def first_kernel(
    state_ref, index_ref, fill_ref, out_ref, table_ref, list_ref, held_ref, index_held_ref, sems, *, nodes, fdev
):
    copy = pltpu.make_async_copy(state_ref.at[pl.ds(0, 3 * nodes)], held_ref, sems.at[0])
    index_copy = pltpu.make_async_copy(index_ref.at[0], index_held_ref, sems.at[1])
    copy.start()
    index_copy.start()
    index_copy.wait()
    copy.wait()
    store_table(table_ref, held_ref[...], nodes)
    send_gather(table_ref, index_held_ref, fill_ref, out_ref, list_ref, 0, nodes, fdev)


def local_kernel(
    state_ref, coef_ref, cross_ref, index_ref,
    local_ref, inv_ref, elim_ref, rot_ref, up_ref, down_ref,
    table_ref, rows_ref, hold_ref, *, nodes, fdev,
):
    half_rows = 3 * nodes
    groups, lines, _ = local_ref.shape
    blocks = lines // 3
    coef = coef_ref[...]
    folded = fold_coef(coef, 3)
    fold(state_ref[half_rows:], rows_ref)
    store_table(table_ref, state_ref[:half_rows], nodes)

    def chores():
        yield from factor_steps(folded, inv_ref, elim_ref)
        sparse, close = strided(rows_ref, folded.shape[0], nodes), dense(hold_ref)
        for step in range(STEPS):
            get = sparse[0] if step == 0 else close[0]
            put = sparse[1] if step == STEPS - 1 else close[1]
            yield from solve_steps(get, put, hold_ref, folded, inv_ref, elim_ref, nodes)

    steps = chores()
    chunks = groups * blocks // CHUNK
    share = -(-(nodes // 2 + STEPS * nodes) // chunks)
    for i in range(chunks):
        ids = [i * CHUNK + k for k in range(CHUNK)]
        index = index_chunk(index_ref.at[0], ids, groups, blocks)
        rows = gather_row(table_ref[...], index, nodes, fdev, lambda: run(steps, share))
        put_chunk(local_ref, ids, rows, blocks)
    run(steps)

    rot_ref[...] = unfold(rows_ref, half_rows)
    cross_hot = hot(cross_ref[pl.ds(0, 1), :], fdev)
    leave(rot_ref[...], coef, cross_hot, up_ref, down_ref)


def leave(rot, coef, cross_hot, up_ref, down_ref):
    up, down = pack(pick(rot, cross_hot))
    rows = up.shape[0]
    up_ref[:rows] = up
    down_ref[:rows] = down
    moved = pick(jnp.broadcast_to(coef, (8, coef.shape[1])), cross_hot)
    up_ref[rows:] = moved
    down_ref[rows:] = pltpu.roll(moved, moved.shape[1] // 2, 1)


def local_next_kernel(
    state_ref, up_ref, down_ref, rot_ref, coef_ref, cross_ref, index_ref, told_ref,
    local_ref, inv_ref, elim_ref, rot_out_ref, coef_out_ref, rup_ref, rdown_ref,
    table_ref, list_ref, *, step, nodes, fdev,
):
    groups, lines, _ = local_ref.shape
    blocks = lines // 3
    part = 3 * nodes // 2
    words = live_words(told_ref, blocks, BLOCK // 2)
    count = list_live(lambda g, b: (words[g] >> b) & 1, list_ref, groups, blocks)
    local_ref[...] = jnp.zeros_like(local_ref)
    cross_hot = hot(cross_ref[pl.ds(step - 1, 1), :], fdev)
    keep = kept(cross_hot)
    rows = pl.ds(3 * nodes, 8)
    first, _ = unpack(up_ref[rows, :], down_ref[rows, :])
    coef = jnp.where(keep, coef_ref[...], place(first, cross_hot)[0:1])
    coef_out_ref[...] = coef
    store_table(table_ref, state_ref[...], nodes)
    run(factor_steps(fold_coef(coef, 3), inv_ref, elim_ref))
    rot = arrive(up_ref, down_ref, rot_ref[...], cross_hot, keep, part)
    rot_out_ref[...] = rot
    leave(rot, coef, hot(cross_ref[pl.ds(step, 1), :], fdev), rup_ref, rdown_ref)
    gather_live(table_ref, index_ref.at[step], local_ref, list_ref, count, groups, blocks, nodes, fdev)


def contact_kernel(
    got_ref, local_ref, index_ref, state_ref, coef_ref, inv_ref, elim_ref, cross_ref, rup_ref, rdown_ref,
    pos_ref, up_ref, down_ref,
    acc_ref, rows_ref, hold_ref, force_ref, list_ref, *, step, nodes, fdev,
):
    half_rows = 3 * nodes
    groups, lines, _ = local_ref.shape
    blocks = lines // 3
    pairs = groups * blocks
    acc_ref[...] = jnp.zeros_like(acc_ref)
    force_ref[:, pairs:] = jnp.zeros_like(force_ref[:, pairs:])
    lanes = lax.broadcasted_iota(jnp.int32, (blocks, BLOCK), 1).astype(F32)
    words = live_words(got_ref, blocks, 0)
    for g in range(groups):
        delta = [
            got_ref[g, c * blocks : (c + 1) * blocks] - local_ref[g, c * blocks : (c + 1) * blocks] for c in range(3)
        ]
        radius = delta[0] * delta[0] + delta[1] * delta[1] + delta[2] * delta[2]
        live = lanes < got_ref[g, 3 * blocks :, 0:1]
        scale = 1.0 / (1.0 + radius)
        for c in range(3):
            force_ref[c, g * blocks : (g + 1) * blocks] = jnp.where(live, delta[c] * scale, 0.0)
    count = list_live(lambda g, b: (words[g] >> b) & 1, list_ref, groups, blocks)
    wide = fdev // LANES
    keys = wide * nodes

    @pl.loop(0, (count + CHUNK - 1) // CHUNK)
    def _(i):
        ids = [jnp.where(i * CHUNK + k < count, list_ref[i * CHUNK + k], pairs) for k in range(CHUNK)]
        index = index_chunk(index_ref.at[step], [jnp.minimum(n, pairs - 1) for n in ids], groups, blocks)
        lane, per_node = parts_of(index, nodes)
        key = row_key(per_node, nodes, fdev)
        mask = lax.broadcasted_iota(jnp.int32, (keys, index.shape[1]), 0) == key
        highs, lows = [], []
        for c in range(3):
            force = jnp.concatenate([force_ref[c, pl.ds(n, 1), :] for n in ids], axis=1)
            hi, lo = split2(force)
            highs.append(jnp.where(mask, hi.astype(F32), 0.0).astype(BF16))
            lows.append(jnp.where(mask, lo.astype(F32), 0.0).astype(BF16))
        spread = jnp.concatenate(highs + lows, axis=0)
        acc_ref[...] += dot_nt(spread, hot(lane, LANES))

    total = acc_ref[: 3 * keys] + acc_ref[3 * keys :]
    contact = jnp.concatenate(
        [
            jnp.concatenate([total[(c * wide + w) * nodes : (c * wide + w + 1) * nodes] for c in range(3)], axis=0)
            for w in range(wide)
        ],
        axis=1,
    )
    fold(state_ref[:half_rows] + 0.5 * contact, rows_ref)
    folded = fold_coef(coef_ref[...], 3)
    get, put = strided(rows_ref, folded.shape[0], nodes)
    run(solve_steps(get, put, hold_ref, folded, inv_ref, elim_ref, nodes))
    pos_ref[...] = unfold(rows_ref, half_rows)
    up, down = pack(pick(pos_ref[...], hot(cross_ref[pl.ds(step, 1), :], fdev)))
    rows = up.shape[0]
    up_ref[:rows] = up
    down_ref[:rows] = down
    up_ref[rows:] = rup_ref[...]
    down_ref[rows:] = rdown_ref[...]


def kept(cross_hot):
    ones = jnp.ones((8, cross_hot.shape[1]), BF16)
    return dot_nt(ones, cross_hot)[0:1] < 0.5


def arrive(up_ref, down_ref, values, cross_hot, keep, at):
    rows = pl.ds(at, values.shape[0] // 2)
    first, second = unpack(up_ref[rows, :], down_ref[rows, :])
    return jnp.where(keep, values, place(jnp.concatenate([first, second], axis=0), cross_hot))


def next_kernel(
    up_ref, down_ref, pos_ref, cross_ref, index_ref, fill_ref,
    state_ref, out_ref,
    table_ref, list_ref, *, step, nodes, fdev,
):
    cross_hot = hot(cross_ref[pl.ds(step - 1, 1), :], fdev)
    positions = arrive(up_ref, down_ref, pos_ref[...], cross_hot, kept(cross_hot), 0)
    state_ref[...] = positions
    store_table(table_ref, positions, nodes)
    send_gather(table_ref, index_ref.at[step], fill_ref, out_ref, list_ref, step, nodes, fdev)


def last_kernel(up_ref, down_ref, pos_ref, rot_ref, cross_ref, state_ref, *, step, nodes, fdev):
    rows = 3 * nodes
    cross_hot = hot(cross_ref[pl.ds(step, 1), :], fdev)
    keep = kept(cross_hot)
    state_ref[:rows] = arrive(up_ref, down_ref, pos_ref[...], cross_hot, keep, 0)
    state_ref[rows:] = arrive(up_ref, down_ref, rot_ref[...], cross_hot, keep, rows // 2)


def shifted(block, axis, distance):
    devices = range(lax.axis_size(axis))
    route = [((i - distance) % len(devices), i) for i in devices]
    return lax.ppermute(block, axis, route)


def per_device(state, stiffness, crossing, contact_send, contact_recv, contact_fill):
    fields, nodes, fdev = state.shape
    _, groups, quota = contact_send.shape
    blocks = quota // BLOCK
    pairs = groups * blocks
    cross = crossing.shape[1]
    rows = 3 * nodes
    moved = rows + 8
    lines = 3 * fdev // BLOCK
    vmem = pl.BlockSpec(memory_space=pltpu.VMEM)
    smem = pl.BlockSpec(memory_space=pltpu.SMEM)
    hbm = pl.BlockSpec(memory_space=pltpu.HBM)
    table = pltpu.VMEM((2 * rows * fdev // LANES, LANES), BF16)
    listed = pltpu.SMEM((pairs + 1,), jnp.int32)
    folded = pltpu.VMEM((lines * nodes, BLOCK), F32)

    def sds(*shape):
        return jax.ShapeDtypeStruct(shape, F32)

    sent_shape = sds(groups, 4 * blocks, BLOCK)
    factors = sds(nodes // 2, lines, BLOCK)

    hold = pltpu.VMEM((nodes, lines, BLOCK), F32)

    def call(kernel, name, ins, outs, scratch, flops, limit=VMEM_LIMIT, **static):
        return pl.pallas_call(
            functools.partial(kernel, nodes=nodes, fdev=fdev, **static),
            out_shape=outs,
            in_specs=ins,
            out_specs=[vmem] * len(outs),
            scratch_shapes=scratch,
            name=name,
            cost_estimate=pl.CostEstimate(flops=flops, bytes_accessed=4 * fields * nodes * fdev, transcendentals=0),
            compiler_params=pltpu.CompilerParams(vmem_limit_bytes=limit),
        )

    def by_block(index):
        return index.reshape(-1, groups, blocks, BLOCK).transpose(0, 2, 1, 3).reshape(-1, pairs, BLOCK)

    send, recv = by_block(contact_send), by_block(contact_recv)
    matmul = 2 * 2 * rows * fdev * groups * quota
    xcur = state.reshape(fields * nodes, fdev)
    coef = stiffness.reshape(1, fdev)
    (sent,) = call(
        first_kernel, "send_first", [hbm, hbm, smem], [sent_shape],
        [table, listed, pltpu.VMEM((rows, fdev), F32), pltpu.VMEM((pairs, BLOCK), jnp.int32),
         pltpu.SemaphoreType.DMA((2,))], matmul, limit=FIRST_LIMIT,
    )(xcur, send, contact_fill)
    got_shape = sds(groups, 3 * blocks, BLOCK)
    rot_moved = sds(rows // 2 + 8, cross)
    for step in range(STEPS):
        told = None if step == 0 else got
        got = lax.all_to_all(sent, "span", split_axis=0, concat_axis=0, tiled=True)
        if step == 0:
            local, inv, elim, rot, rup, rdown = call(
                local_kernel, "local", [vmem] * 4,
                [got_shape, factors, factors, sds(rows, fdev), rot_moved, rot_moved],
                [table, folded, hold], matmul,
            )(xcur, coef, crossing, recv)
        else:
            local, inv, elim, rot, coef, rup, rdown = call(
                local_next_kernel, "local_next", [vmem] * 8,
                [got_shape, factors, factors, sds(rows, fdev), sds(1, fdev), rot_moved, rot_moved],
                [table, listed], matmul, step=step,
            )(xcur, up, down, rot, coef, crossing, recv, told)
        pos, up, down = call(
            contact_kernel, "contact", [vmem] * 10,
            [sds(rows, fdev), sds(moved, cross), sds(moved, cross)],
            [pltpu.VMEM((2 * rows * fdev // LANES, LANES), F32), folded, hold,
             pltpu.VMEM((3, pairs + 8, BLOCK), F32), listed], matmul, step=step,
        )(got, local, recv, xcur, coef, inv, elim, crossing, rup, rdown)
        up = shifted(up, "stream", 1)
        down = shifted(down, "stream", -1)
        if step + 1 < STEPS:
            xcur, sent = call(
                next_kernel, "send_next", [vmem] * 5 + [smem],
                [sds(rows, fdev), sent_shape], [table, listed], matmul, step=step + 1,
            )(up, down, pos, crossing, send, contact_fill)
        else:
            (xcur,) = call(last_kernel, "arrive", [vmem] * 5, [sds(fields * nodes, fdev)], [], matmul // 8, step=step)(
                up, down, pos, rot, crossing
            )
    return xcur.reshape(fields, nodes, fdev)


def solution(mesh):
    placed = (
        P(None, None, ("span", "stream")),
        P(("span", "stream")),
        P(None, ("span", "stream")),
        P(None, None, ("span", "stream")),
        P(None, None, ("span", "stream")),
        P(None, None, ("span", "stream")),
    )
    return jax.shard_map(
        per_device,
        mesh=mesh,
        in_specs=placed,
        out_specs=P(None, None, ("span", "stream")),
        check_vma=False,
    )
```

```python
import functools

import jax
import jax.numpy as jnp
from jax import lax
from jax.experimental import pallas as pl
from jax.experimental.pallas import tpu as pltpu
from jax.sharding import PartitionSpec as P

STEPS = 2
BLOCK = 128
LANES = 256
CHUNK = 8
PAD = 8
F32 = jnp.float32
BF16 = jnp.bfloat16
VMEM_LIMIT = 48 * 1024 * 1024
FIRST_LIMIT = 63 * 1024 * 1024


def split2(x):
    hi = x.astype(BF16)
    lo = (x - hi.astype(F32)).astype(BF16)
    return hi, lo


def split3(x):
    hi = x.astype(BF16)
    rest = x - hi.astype(F32)
    mid = rest.astype(BF16)
    lo = (rest - mid.astype(F32)).astype(BF16)
    return hi, mid, lo


def hot(index, count):
    rows = lax.broadcasted_iota(jnp.int32, (count, index.shape[1]), 0)
    return jnp.where(rows == index, 1.0, 0.0).astype(BF16)


def dot_nt(a, b):
    return lax.dot_general(a, b, (((1,), (1,)), ((), ())), preferred_element_type=F32)


def parts_of(index, nodes):
    per_node = index >> (LANES.bit_length() - 1)
    lane = index & (LANES - 1)
    return lane, per_node


def row_key(per_node, nodes, fdev):
    wide = fdev // LANES
    return (per_node & (wide - 1)) * nodes + (per_node >> (wide.bit_length() - 1))


def store_table(table_ref, positions, nodes):
    wide = positions.shape[1] // LANES
    rows = 3 * wide * nodes
    for c in range(3):
        for w in range(wide):
            hi, lo = split2(positions[c * nodes : (c + 1) * nodes, w * LANES : (w + 1) * LANES])
            at = (c * wide + w) * nodes
            table_ref[at : at + nodes] = hi
            table_ref[rows + at : rows + at + nodes] = lo


def gather_row(table, index, nodes, fdev, between=lambda: None):
    lane, per_node = parts_of(index, nodes)
    got = jnp.dot(table, hot(lane, LANES), preferred_element_type=F32)
    between()
    return select_rows(got, row_key(per_node, nodes, fdev))


def arrived_row(table, slots, index, fdev):
    slot = index & (fdev - 1)
    onto = jnp.where(slots == slot, 1.0, 0.0).astype(BF16)
    got = jnp.dot(table, onto, preferred_element_type=F32)
    return select_rows(got, index >> (fdev.bit_length() - 1))


def select_rows(got, key):
    rows = got.shape[0] // 2
    keys = rows // 3
    relative = key - lax.broadcasted_iota(jnp.int32, (8, key.shape[1]), 0)
    out = []
    for c in range(3):
        acc = jnp.zeros((8, key.shape[1]), F32)
        for j in range(0, keys, 8):
            at = c * keys + j
            acc = jnp.where(relative == j, got[at : at + 8] + got[rows + at : rows + at + 8], acc)
        out.append(jnp.sum(acc, axis=0, keepdims=True))
    return out


def list_live(live_of, list_ref, groups, blocks):
    count = jnp.int32(0)
    for g in range(groups):
        for b in range(blocks):
            list_ref[count] = g * blocks + b
            count = count + live_of(g, b)
    return count


def index_chunk(index_ref, ids, groups, blocks):
    rows = [(n & (blocks - 1)) * groups + (n >> (blocks.bit_length() - 1)) for n in ids]
    return jnp.concatenate([index_ref[pl.ds(n, 1), :] for n in rows], axis=1)


def put_chunk(out_ref, ids, rows, blocks):
    for k, n in enumerate(ids):
        for c in range(3):
            at = c * blocks + (n & (blocks - 1))
            out_ref[n >> (blocks.bit_length() - 1), pl.ds(at, 1), :] = rows[c][:, k * BLOCK : (k + 1) * BLOCK]


def each_chunk(count, body):
    chunks = (count + CHUNK - 1) // CHUNK
    fours = chunks >> 2

    @pl.loop(0, fours)
    def _(i):
        body([i * 4 + k for k in range(4)])

    @pl.when((chunks & 2) > 0)
    def _():
        body([fours * 4, fours * 4 + 1])

    @pl.when((chunks & 1) > 0)
    def _():
        body([chunks - 1])


def gather_live(index_ref, out_ref, list_ref, count, groups, blocks, gather):
    def body(numbers):
        for i in numbers:
            ids = [list_ref[jnp.minimum(i * CHUNK + k, count - 1)] for k in range(CHUNK)]
            put_chunk(out_ref, ids, gather(index_chunk(index_ref, ids, groups, blocks)), blocks)

    each_chunk(count, body)


def get_chunk(ref, ids, blocks):
    shift = blocks.bit_length() - 1
    return [
        jnp.concatenate([ref[n >> shift, pl.ds(c * blocks + (n & (blocks - 1)), 1), :] for n in ids], axis=1)
        for c in range(3)
    ]


def send_start(fill_ref, out_ref, list_ref, step):
    groups, lines, _ = out_ref.shape
    blocks = lines // 4
    low = lax.broadcasted_iota(jnp.int32, (1, BLOCK), 1) < BLOCK // 2
    out_ref[...] = jnp.zeros_like(out_ref)
    for g in range(groups):
        for b in range(blocks):
            fills = jnp.where(low, fill_ref[step, g, b], fill_ref[STEPS - 1, g, b])
            out_ref[g, pl.ds(3 * blocks + b, 1), :] = fills.astype(F32)
    return list_live(lambda g, b: (fill_ref[step, g, b] > 0).astype(jnp.int32), list_ref, groups, blocks)


def send_gather(table_ref, index_ref, out_ref, list_ref, count, nodes, fdev):
    groups, lines, _ = out_ref.shape
    gather_live(
        index_ref, out_ref, list_ref, count, groups, lines // 4,
        lambda index: gather_row(table_ref[...], index, nodes, fdev),
    )


def live_words(got_ref, blocks, lane):
    sub = lax.broadcasted_iota(jnp.int32, (blocks, BLOCK), 0)
    here = lax.broadcasted_iota(jnp.int32, (blocks, BLOCK), 1) == lane
    words = []
    for g in range(got_ref.shape[0]):
        live = (got_ref[g, 3 * blocks :] > 0.5) & here
        words.append(jnp.sum(jnp.where(live, jnp.left_shift(1, sub), 0).astype(F32)).astype(jnp.int32))
    return words


def fold(values, rows_ref, nodes):
    fields = values.shape[0] // nodes
    pitch = nodes + PAD
    for i in range(values.shape[1] // BLOCK):
        for c in range(fields):
            at = (i * fields + c) * pitch
            rows_ref[at : at + nodes] = values[c * nodes : (c + 1) * nodes, i * BLOCK : (i + 1) * BLOCK]


def unfold(rows_ref, rows, nodes):
    fields = rows // nodes
    pitch = nodes + PAD
    lines = rows_ref.shape[0] // pitch
    runs = [rows_ref[k * pitch : k * pitch + nodes] for k in range(lines)]
    return jnp.concatenate(
        [jnp.concatenate(runs[i : i + fields], axis=0) for i in range(0, lines, fields)], axis=1
    )


def fold_coef(coef, fields):
    chunks = coef.shape[1] // BLOCK
    return jnp.concatenate(
        [jnp.broadcast_to(coef[:, i * BLOCK : (i + 1) * BLOCK], (fields, BLOCK)) for i in range(chunks)], axis=0
    )


def factor_steps(coef, inv_ref, elim_ref):
    inv = 1.0 / (1.0 + coef)
    for k in range(inv_ref.shape[0]):
        if k:
            inv = 1.0 / (1.0 + 2.0 * coef - coef * elim)
        elim = coef * inv
        inv_ref[k] = inv
        elim_ref[k] = elim
        yield


def solve_steps(get, put, hold_ref, coef, inv_ref, elim_ref, nodes):
    half = nodes // 2
    top = get(0) * inv_ref[0]
    bot = get(nodes - 1) * inv_ref[0]
    hold_ref[0] = top
    hold_ref[nodes - 1] = bot
    for k in range(1, half - 1):
        inv = inv_ref[k]
        elim = elim_ref[k]
        top = get(k) * inv + elim * top
        bot = get(nodes - 1 - k) * inv + elim * bot
        hold_ref[k] = top
        hold_ref[nodes - 1 - k] = bot
        yield
    left = get(half - 1) + coef * top
    right = get(half) + coef * bot
    pivot = 1.0 + 2.0 * coef - coef * elim_ref[half - 2]
    even = (left + right) * (0.5 / (pivot - coef))
    odd = (left - right) * (0.5 / (pivot + coef))
    top, bot = even + odd, even - odd
    put(half - 1, top)
    put(half, bot)
    yield
    for k in range(half - 2, -1, -1):
        elim = elim_ref[k]
        top = hold_ref[k] + elim * top
        bot = hold_ref[nodes - 1 - k] + elim * bot
        put(k, top)
        put(nodes - 1 - k, bot)
        yield


def strided(rows_ref, lines, nodes):
    def get(n):
        return rows_ref[pl.ds(n, lines, stride=nodes + PAD), :]

    def put(n, value):
        rows_ref[pl.ds(n, lines, stride=nodes + PAD), :] = value

    return get, put


def dense(hold_ref):
    def get(n):
        return hold_ref[n]

    def put(n, value):
        hold_ref[n] = value

    return get, put


def run(steps, count=None):
    done = 0
    while count is None or done < count:
        if next(steps, steps) is steps:
            return
        done += 1


def pick(values, cross_hot):
    rows = values.shape[0]
    got = jnp.dot(jnp.concatenate(split3(values), axis=0), cross_hot, preferred_element_type=F32)
    return (got[:rows] + got[rows : 2 * rows]) + got[2 * rows :]


def place(values, cross_hot):
    rows = values.shape[0]
    got = dot_nt(jnp.concatenate(split3(values), axis=0), cross_hot)
    return (got[:rows] + got[rows : 2 * rows]) + got[2 * rows :]


def pack(leavers):
    rows = leavers.shape[0] // 2
    half = leavers.shape[1] // 2
    first, second = leavers[:rows], leavers[rows:]
    low = lax.broadcasted_iota(jnp.int32, first.shape, 1) < half
    up = jnp.where(low, first, pltpu.roll(second, half, 1))
    down = jnp.where(low, pltpu.roll(first, half, 1), second)
    return up, down


def unpack(up, down):
    half = up.shape[1] // 2
    low = lax.broadcasted_iota(jnp.int32, up.shape, 1) < half
    first = jnp.where(low, up, pltpu.roll(down, half, 1))
    second = jnp.where(low, pltpu.roll(up, half, 1), down)
    return first, second


def first_kernel(
    state_ref, index_ref, fill_ref, out_ref,
    table_ref, list_ref, held_ref, index_held_ref, fill_held_ref, sems, *, nodes, fdev
):
    pairs = (
        (fill_ref, fill_held_ref),
        (state_ref.at[pl.ds(0, 3 * nodes)], held_ref),
        (index_ref.at[0], index_held_ref),
    )
    copies = [pltpu.make_async_copy(src, dst, sems.at[i]) for i, (src, dst) in enumerate(pairs)]
    for copy in copies:
        copy.start()
    copies[0].wait()
    count = send_start(fill_held_ref, out_ref, list_ref, 0)
    copies[1].wait()
    store_table(table_ref, held_ref[...], nodes)
    copies[2].wait()
    send_gather(table_ref, index_held_ref, out_ref, list_ref, count, nodes, fdev)


def local_kernel(
    state_ref, coef_ref, cross_ref, index_ref,
    local_ref, inv_ref, elim_ref, rot_ref, up_ref, down_ref,
    table_ref, rows_ref, hold_ref, *, nodes, fdev,
):
    half_rows = 3 * nodes
    groups, lines, _ = local_ref.shape
    blocks = lines // 3
    coef = coef_ref[...]
    folded = fold_coef(coef, 3)
    fold(state_ref[half_rows:], rows_ref, nodes)
    store_table(table_ref, state_ref[:half_rows], nodes)

    def chores():
        yield from factor_steps(folded, inv_ref, elim_ref)
        sparse, close = strided(rows_ref, folded.shape[0], nodes), dense(hold_ref)
        for step in range(STEPS):
            get = sparse[0] if step == 0 else close[0]
            put = sparse[1] if step == STEPS - 1 else close[1]
            yield from solve_steps(get, put, hold_ref, folded, inv_ref, elim_ref, nodes)

    steps = chores()
    chunks = groups * blocks // CHUNK
    share = -(-(nodes // 2 + STEPS * nodes) // chunks)
    for i in range(chunks):
        ids = [i * CHUNK + k for k in range(CHUNK)]
        index = index_chunk(index_ref.at[0], ids, groups, blocks)
        rows = gather_row(table_ref[...], index, nodes, fdev, lambda: run(steps, share))
        put_chunk(local_ref, ids, rows, blocks)
    run(steps)

    rot_ref[...] = unfold(rows_ref, half_rows, nodes)
    cross_hot = hot(cross_ref[pl.ds(0, 1), :], fdev)
    leave(rot_ref[...], coef, cross_hot, up_ref, down_ref)


def leave(rot, coef, cross_hot, up_ref, down_ref):
    up, down = pack(pick(rot, cross_hot))
    rows = up.shape[0]
    up_ref[:rows] = up
    down_ref[:rows] = down
    moved = pick(jnp.broadcast_to(coef, (8, coef.shape[1])), cross_hot)
    up_ref[rows:] = moved
    down_ref[rows:] = pltpu.roll(moved, moved.shape[1] // 2, 1)


def local_next_kernel(
    up_ref, down_ref, pos_ref, rot_ref, coef_ref, cross_ref, index_ref, told_ref,
    state_ref, local_ref, inv_ref, elim_ref, rot_out_ref, coef_out_ref, rup_ref, rdown_ref,
    table_ref, list_ref, *, step, nodes, fdev,
):
    groups, lines, _ = local_ref.shape
    blocks = lines // 3
    part = 3 * nodes // 2
    words = live_words(told_ref, blocks, BLOCK // 2)
    count = list_live(lambda g, b: (words[g] >> b) & 1, list_ref, groups, blocks)
    local_ref[...] = jnp.zeros_like(local_ref)
    cross_hot = hot(cross_ref[pl.ds(step - 1, 1), :], fdev)
    keep = kept(cross_hot)
    rows = pl.ds(3 * nodes, 8)
    first, _ = unpack(up_ref[rows, :], down_ref[rows, :])
    coef = jnp.where(keep, coef_ref[...], place(first, cross_hot)[0:1])
    coef_out_ref[...] = coef
    positions = arrive(up_ref, down_ref, pos_ref[...], cross_hot, keep, 0)
    state_ref[...] = positions
    store_table(table_ref, positions, nodes)
    run(factor_steps(fold_coef(coef, 3), inv_ref, elim_ref))
    rot = arrive(up_ref, down_ref, rot_ref[...], cross_hot, keep, part)
    rot_out_ref[...] = rot
    leave(rot, coef, hot(cross_ref[pl.ds(step, 1), :], fdev), rup_ref, rdown_ref)
    gather_live(
        index_ref.at[step], local_ref, list_ref, count, groups, blocks,
        lambda index: gather_row(table_ref[...], index, nodes, fdev),
    )


def contact_kernel(
    got_ref, local_ref, index_ref, state_ref, coef_ref, inv_ref, elim_ref, cross_ref, rup_ref, rdown_ref,
    pos_ref, up_ref, down_ref,
    acc_ref, rows_ref, hold_ref, force_ref, list_ref, *, step, nodes, fdev,
):
    half_rows = 3 * nodes
    groups, lines, _ = local_ref.shape
    blocks = lines // 3
    pairs = groups * blocks
    acc_ref[...] = jnp.zeros_like(acc_ref)
    force_ref[:, pairs:] = jnp.zeros_like(force_ref[:, pairs:])
    lanes = lax.broadcasted_iota(jnp.int32, (blocks, BLOCK), 1).astype(F32)
    words = live_words(got_ref, blocks, 0)
    for g in range(groups):
        delta = [
            got_ref[g, c * blocks : (c + 1) * blocks] - local_ref[g, c * blocks : (c + 1) * blocks] for c in range(3)
        ]
        radius = delta[0] * delta[0] + delta[1] * delta[1] + delta[2] * delta[2]
        live = lanes < got_ref[g, 3 * blocks :, 0:1]
        scale = 1.0 / (1.0 + radius)
        for c in range(3):
            force_ref[c, g * blocks : (g + 1) * blocks] = jnp.where(live, delta[c] * scale, 0.0)
    count = list_live(lambda g, b: (words[g] >> b) & 1, list_ref, groups, blocks)
    wide = fdev // LANES
    keys = wide * nodes

    def scattered(i):
        ids = [jnp.where(i * CHUNK + k < count, list_ref[i * CHUNK + k], pairs) for k in range(CHUNK)]
        index = index_chunk(index_ref.at[step], [jnp.minimum(n, pairs - 1) for n in ids], groups, blocks)
        lane, per_node = parts_of(index, nodes)
        key = row_key(per_node, nodes, fdev)
        mask = lax.broadcasted_iota(jnp.int32, (keys, index.shape[1]), 0) == key
        highs, lows = [], []
        for c in range(3):
            force = jnp.concatenate([force_ref[c, pl.ds(n, 1), :] for n in ids], axis=1)
            hi, lo = split2(force)
            highs.append(jnp.where(mask, hi.astype(F32), 0.0).astype(BF16))
            lows.append(jnp.where(mask, lo.astype(F32), 0.0).astype(BF16))
        spread = jnp.concatenate(highs + lows, axis=0)
        return dot_nt(spread, hot(lane, LANES))

    def body(numbers):
        total = scattered(numbers[0])
        for i in numbers[1:]:
            total = total + scattered(i)
        acc_ref[...] += total

    each_chunk(count, body)

    total = acc_ref[: 3 * keys] + acc_ref[3 * keys :]
    contact = jnp.concatenate(
        [
            jnp.concatenate([total[(c * wide + w) * nodes : (c * wide + w + 1) * nodes] for c in range(3)], axis=0)
            for w in range(wide)
        ],
        axis=1,
    )
    fold(state_ref[:half_rows] + 0.5 * contact, rows_ref, nodes)
    folded = fold_coef(coef_ref[...], 3)
    get, put = strided(rows_ref, folded.shape[0], nodes)
    run(solve_steps(get, put, hold_ref, folded, inv_ref, elim_ref, nodes))
    pos_ref[...] = unfold(rows_ref, half_rows, nodes)
    up, down = pack(pick(pos_ref[...], hot(cross_ref[pl.ds(step, 1), :], fdev)))
    rows = up.shape[0]
    up_ref[:rows] = up
    down_ref[:rows] = down
    up_ref[rows:] = rup_ref[...]
    down_ref[rows:] = rdown_ref[...]


def kept(cross_hot):
    ones = jnp.ones((8, cross_hot.shape[1]), BF16)
    return dot_nt(ones, cross_hot)[0:1] < 0.5


def arrive(up_ref, down_ref, values, cross_hot, keep, at):
    rows = pl.ds(at, values.shape[0] // 2)
    first, second = unpack(up_ref[rows, :], down_ref[rows, :])
    return jnp.where(keep, values, place(jnp.concatenate([first, second], axis=0), cross_hot))


def own_kernel(
    pos_ref, cross_ref, index_ref, fill_ref, out_ref, table_ref, list_ref, fill_held_ref, sem, *, step, nodes, fdev
):
    copy = pltpu.make_async_copy(fill_ref, fill_held_ref, sem)
    copy.start()
    keep = kept(hot(cross_ref[pl.ds(step - 1, 1), :], fdev))
    store_table(table_ref, jnp.where(keep, pos_ref[...], 0.0), nodes)
    copy.wait()
    count = send_start(fill_held_ref, out_ref, list_ref, step)
    send_gather(table_ref, index_ref.at[step], out_ref, list_ref, count, nodes, fdev)


def next_kernel(
    up_ref, down_ref, own_ref, cross_ref, index_ref, out_ref, table_ref, list_ref, *, step, nodes, fdev
):
    groups, lines, _ = out_ref.shape
    blocks = lines // 4
    words = live_words(own_ref, blocks, 0)
    count = list_live(lambda g, b: (words[g] >> b) & 1, list_ref, groups, blocks)
    out_ref[...] = own_ref[...]
    cross = cross_ref[pl.ds(step - 1, 1), :]
    moved = cross.shape[1]
    here = lax.broadcasted_iota(jnp.int32, (moved, moved), 0) == lax.broadcasted_iota(jnp.int32, (moved, moved), 1)
    slots = jnp.sum(jnp.where(here, cross.astype(F32), 0.0), axis=1, keepdims=True).astype(jnp.int32)
    part = 3 * nodes // 2
    first, second = unpack(up_ref[:part, :], down_ref[:part, :])
    hi, lo = split2(jnp.concatenate([first, second], axis=0))
    table_ref[: 2 * part] = hi
    table_ref[2 * part :] = lo

    def body(numbers):
        for i in numbers:
            ids = [list_ref[jnp.minimum(i * CHUNK + k, count - 1)] for k in range(CHUNK)]
            rows = arrived_row(table_ref[...], slots, index_chunk(index_ref.at[step], ids, groups, blocks), fdev)
            held = get_chunk(own_ref, ids, blocks)
            put_chunk(out_ref, ids, [a + b for a, b in zip(held, rows)], blocks)

    each_chunk(count, body)


def last_kernel(up_ref, down_ref, pos_ref, rot_ref, cross_ref, state_ref, done_ref, sems, *, step, nodes, fdev):
    rows = 3 * nodes
    cross_hot = hot(cross_ref[pl.ds(step, 1), :], fdev)
    keep = kept(cross_hot)
    copies = []
    for i, ref in enumerate((pos_ref, rot_ref)):
        side = pl.ds(i * rows, rows)
        done_ref[side, :] = arrive(up_ref, down_ref, ref[...], cross_hot, keep, i * rows // 2)
        copies.append(pltpu.make_async_copy(done_ref.at[side], state_ref.at[side], sems.at[i]))
        copies[i].start()
    for copy in copies:
        copy.wait()


def shifted(block, axis, distance):
    devices = range(lax.axis_size(axis))
    route = [((i - distance) % len(devices), i) for i in devices]
    return lax.ppermute(block, axis, route)


def per_device(state, stiffness, crossing, contact_send, contact_recv, contact_fill):
    fields, nodes, fdev = state.shape
    _, groups, quota = contact_send.shape
    blocks = quota // BLOCK
    pairs = groups * blocks
    cross = crossing.shape[1]
    rows = 3 * nodes
    moved = rows + 8
    lines = 3 * fdev // BLOCK
    vmem = pl.BlockSpec(memory_space=pltpu.VMEM)
    hbm = pl.BlockSpec(memory_space=pltpu.HBM)
    table = pltpu.VMEM((2 * rows * fdev // LANES, LANES), BF16)
    listed = pltpu.SMEM((pairs + 1,), jnp.int32)
    folded = pltpu.VMEM((lines * (nodes + PAD), BLOCK), F32)

    def sds(*shape):
        return jax.ShapeDtypeStruct(shape, F32)

    sent_shape = sds(groups, 4 * blocks, BLOCK)
    factors = sds(nodes // 2, lines, BLOCK)

    fills = pltpu.SMEM(contact_fill.shape, jnp.int32)
    hold = pltpu.VMEM((nodes, lines, BLOCK), F32)

    def call(kernel, name, ins, outs, scratch, flops, limit=VMEM_LIMIT, space=vmem, **static):
        return pl.pallas_call(
            functools.partial(kernel, nodes=nodes, fdev=fdev, **static),
            out_shape=outs,
            in_specs=ins,
            out_specs=[space] * len(outs),
            scratch_shapes=scratch,
            name=name,
            cost_estimate=pl.CostEstimate(flops=flops, bytes_accessed=4 * fields * nodes * fdev, transcendentals=0),
            compiler_params=pltpu.CompilerParams(vmem_limit_bytes=limit),
        )

    def by_block(index):
        return index.reshape(-1, groups, blocks, BLOCK).transpose(0, 2, 1, 3).reshape(-1, pairs, BLOCK)

    send, recv = by_block(contact_send), by_block(contact_recv)
    matmul = 2 * 2 * rows * fdev * groups * quota
    xcur = state.reshape(fields * nodes, fdev)
    coef = stiffness.reshape(1, fdev)
    (sent,) = call(
        first_kernel, "send_first", [hbm] * 3, [sent_shape],
        [table, listed, pltpu.VMEM((rows, fdev), F32), pltpu.VMEM((pairs, BLOCK), jnp.int32),
         fills, pltpu.SemaphoreType.DMA((3,))], matmul, limit=FIRST_LIMIT,
    )(xcur, send, contact_fill)
    got_shape = sds(groups, 3 * blocks, BLOCK)
    rot_moved = sds(rows // 2 + 8, cross)
    for step in range(STEPS):
        told = None if step == 0 else got
        got = lax.all_to_all(sent, "span", split_axis=0, concat_axis=0, tiled=True)
        if step == 0:
            local, inv, elim, rot, rup, rdown = call(
                local_kernel, "local", [vmem] * 4,
                [got_shape, factors, factors, sds(rows, fdev), rot_moved, rot_moved],
                [table, folded, hold], matmul,
            )(xcur, coef, crossing, recv)
        else:
            xcur, local, inv, elim, rot, coef, rup, rdown = call(
                local_next_kernel, "local_next", [vmem] * 8,
                [sds(rows, fdev), got_shape, factors, factors, sds(rows, fdev), sds(1, fdev), rot_moved, rot_moved],
                [table, listed], matmul, step=step,
            )(up, down, pos, rot, coef, crossing, recv, told)
        pos, up, down = call(
            contact_kernel, "contact", [vmem] * 10,
            [sds(rows, fdev), sds(moved, cross), sds(moved, cross)],
            [pltpu.VMEM((2 * rows * fdev // LANES, LANES), F32), folded, hold,
             pltpu.VMEM((3, pairs + 8, BLOCK), F32), listed], matmul, step=step,
        )(got, local, recv, xcur, coef, inv, elim, crossing, rup, rdown)
        up = shifted(up, "stream", 1)
        down = shifted(down, "stream", -1)
        if step + 1 < STEPS:
            (own,) = call(
                own_kernel, "send_own", [vmem] * 4, [sent_shape],
                [table, listed, fills, pltpu.SemaphoreType.DMA(())], matmul, step=step + 1,
            )(pos, crossing, send, contact_fill)
            (sent,) = call(
                next_kernel, "send_next", [vmem] * 5, [sent_shape],
                [pltpu.VMEM((2 * rows, cross), BF16), listed], matmul, step=step + 1,
            )(up, down, own, crossing, send)
        else:
            (xcur,) = call(
                last_kernel, "arrive", [vmem] * 5, [sds(fields * nodes, fdev)],
                [pltpu.VMEM((fields * nodes, fdev), F32), pltpu.SemaphoreType.DMA((2,))],
                matmul // 8, space=hbm, step=step,
            )(up, down, pos, rot, crossing)
    return xcur.reshape(fields, nodes, fdev)


def solution(mesh):
    placed = (
        P(None, None, ("span", "stream")),
        P(("span", "stream")),
        P(None, ("span", "stream")),
        P(None, None, ("span", "stream")),
        P(None, None, ("span", "stream")),
        P(None, None, ("span", "stream")),
    )
    return jax.shard_map(
        per_device,
        mesh=mesh,
        in_specs=placed,
        out_specs=P(None, None, ("span", "stream")),
        check_vma=False,
    )
```

```python
import functools

import jax
import jax.numpy as jnp
from jax import lax
from jax.experimental import pallas as pl
from jax.experimental.pallas import tpu as pltpu
from jax.sharding import PartitionSpec as P

STEPS = 2
BLOCK = 128
LANES = 256
CHUNK = 8
PAD = 8
F32 = jnp.float32
BF16 = jnp.bfloat16
VMEM_LIMIT = 48 * 1024 * 1024
FIRST_LIMIT = 63 * 1024 * 1024


def split2(x):
    hi = x.astype(BF16)
    lo = (x - hi.astype(F32)).astype(BF16)
    return hi, lo


def split3(x):
    hi = x.astype(BF16)
    rest = x - hi.astype(F32)
    mid = rest.astype(BF16)
    lo = (rest - mid.astype(F32)).astype(BF16)
    return hi, mid, lo


def hot(index, count):
    rows = lax.broadcasted_iota(jnp.int32, (count, index.shape[1]), 0)
    return jnp.where(rows == index, 1.0, 0.0).astype(BF16)


def dot_nt(a, b):
    return lax.dot_general(a, b, (((1,), (1,)), ((), ())), preferred_element_type=F32)


def parts_of(index, nodes):
    per_node = index >> (LANES.bit_length() - 1)
    lane = index & (LANES - 1)
    return lane, per_node


def row_key(per_node, nodes, fdev):
    wide = fdev // LANES
    return (per_node & (wide - 1)) * nodes + (per_node >> (wide.bit_length() - 1))


def store_table(table_ref, positions, nodes):
    wide = positions.shape[1] // LANES
    rows = 3 * wide * nodes
    for c in range(3):
        for w in range(wide):
            hi, lo = split2(positions[c * nodes : (c + 1) * nodes, w * LANES : (w + 1) * LANES])
            at = (c * wide + w) * nodes
            table_ref[at : at + nodes] = hi
            table_ref[rows + at : rows + at + nodes] = lo


def gather_row(table, index, nodes, fdev, between=lambda: None):
    lane, per_node = parts_of(index, nodes)
    got = jnp.dot(table, hot(lane, LANES), preferred_element_type=F32)
    between()
    return select_rows(got, row_key(per_node, nodes, fdev))


def arrived_row(table, slots, index, fdev):
    slot = index & (fdev - 1)
    onto = jnp.where(slots == slot, 1.0, 0.0).astype(BF16)
    got = jnp.dot(table, onto, preferred_element_type=F32)
    return select_rows(got, index >> (fdev.bit_length() - 1))


def select_rows(got, key):
    rows = got.shape[0] // 2
    keys = rows // 3
    relative = key - lax.broadcasted_iota(jnp.int32, (8, key.shape[1]), 0)
    out = []
    for c in range(3):
        acc = jnp.zeros((8, key.shape[1]), F32)
        for j in range(0, keys, 8):
            at = c * keys + j
            acc = jnp.where(relative == j, got[at : at + 8] + got[rows + at : rows + at + 8], acc)
        out.append(jnp.sum(acc, axis=0, keepdims=True))
    return out


def list_live(live_of, list_ref, groups, blocks):
    count = jnp.int32(0)
    for g in range(groups):
        for b in range(blocks):
            list_ref[count] = g * blocks + b
            count = count + live_of(g, b)
    return count


def index_chunk(index_ref, ids, groups, blocks):
    rows = [(n & (blocks - 1)) * groups + (n >> (blocks.bit_length() - 1)) for n in ids]
    return jnp.concatenate([index_ref[pl.ds(n, 1), :] for n in rows], axis=1)


def put_chunk(out_ref, ids, rows, blocks):
    for k, n in enumerate(ids):
        for c in range(3):
            at = c * blocks + (n & (blocks - 1))
            out_ref[n >> (blocks.bit_length() - 1), pl.ds(at, 1), :] = rows[c][:, k * BLOCK : (k + 1) * BLOCK]


def each_chunk(count, body):
    chunks = (count + CHUNK - 1) // CHUNK
    fours = chunks >> 2

    @pl.loop(0, fours)
    def _(i):
        body([i * 4 + k for k in range(4)])

    @pl.when((chunks & 2) > 0)
    def _():
        body([fours * 4, fours * 4 + 1])

    @pl.when((chunks & 1) > 0)
    def _():
        body([chunks - 1])


def gather_live(index_ref, out_ref, list_ref, count, groups, blocks, gather):
    def body(numbers):
        ids = [list_ref[jnp.minimum(i * CHUNK + k, count - 1)] for i in numbers for k in range(CHUNK)]
        put_chunk(out_ref, ids, gather(index_chunk(index_ref, ids, groups, blocks)), blocks)

    each_chunk(count, body)


def get_chunk(ref, ids, blocks):
    shift = blocks.bit_length() - 1
    return [
        jnp.concatenate([ref[n >> shift, pl.ds(c * blocks + (n & (blocks - 1)), 1), :] for n in ids], axis=1)
        for c in range(3)
    ]


def send_start(fill_ref, out_ref, list_ref, step):
    groups, lines, _ = out_ref.shape
    blocks = lines // 4
    low = lax.broadcasted_iota(jnp.int32, (1, BLOCK), 1) < BLOCK // 2
    out_ref[...] = jnp.zeros_like(out_ref)
    for g in range(groups):
        for b in range(blocks):
            fills = jnp.where(low, fill_ref[step, g, b], fill_ref[STEPS - 1, g, b])
            out_ref[g, pl.ds(3 * blocks + b, 1), :] = fills.astype(F32)
    return list_live(lambda g, b: (fill_ref[step, g, b] > 0).astype(jnp.int32), list_ref, groups, blocks)


def send_gather(table_ref, index_ref, out_ref, list_ref, count, nodes, fdev):
    groups, lines, _ = out_ref.shape
    gather_live(
        index_ref, out_ref, list_ref, count, groups, lines // 4,
        lambda index: gather_row(table_ref[...], index, nodes, fdev),
    )


def live_words(got_ref, blocks, lane):
    sub = lax.broadcasted_iota(jnp.int32, (blocks, BLOCK), 0)
    here = lax.broadcasted_iota(jnp.int32, (blocks, BLOCK), 1) == lane
    words = []
    for g in range(got_ref.shape[0]):
        live = (got_ref[g, 3 * blocks :] > 0.5) & here
        words.append(jnp.sum(jnp.where(live, jnp.left_shift(1, sub), 0).astype(F32)).astype(jnp.int32))
    return words


def fold(values, rows_ref, nodes):
    fields = values.shape[0] // nodes
    pitch = nodes + PAD
    for i in range(values.shape[1] // BLOCK):
        for c in range(fields):
            at = (i * fields + c) * pitch
            rows_ref[at : at + nodes] = values[c * nodes : (c + 1) * nodes, i * BLOCK : (i + 1) * BLOCK]


def unfold(rows_ref, rows, nodes):
    fields = rows // nodes
    pitch = nodes + PAD
    lines = rows_ref.shape[0] // pitch
    runs = [rows_ref[k * pitch : k * pitch + nodes] for k in range(lines)]
    return jnp.concatenate(
        [jnp.concatenate(runs[i : i + fields], axis=0) for i in range(0, lines, fields)], axis=1
    )


def fold_coef(coef, fields):
    chunks = coef.shape[1] // BLOCK
    return jnp.concatenate(
        [jnp.broadcast_to(coef[:, i * BLOCK : (i + 1) * BLOCK], (fields, BLOCK)) for i in range(chunks)], axis=0
    )


def factor_steps(coef, inv_ref, elim_ref):
    inv = 1.0 / (1.0 + coef)
    for k in range(inv_ref.shape[0]):
        if k:
            inv = 1.0 / (1.0 + 2.0 * coef - coef * elim)
        elim = coef * inv
        inv_ref[k] = inv
        elim_ref[k] = elim
        yield


def solve_steps(get, put, hold_ref, coef, inv_ref, elim_ref, nodes):
    half = nodes // 2
    top = get(0) * inv_ref[0]
    bot = get(nodes - 1) * inv_ref[0]
    hold_ref[0] = top
    hold_ref[nodes - 1] = bot
    for k in range(1, half - 1):
        inv = inv_ref[k]
        elim = elim_ref[k]
        top = get(k) * inv + elim * top
        bot = get(nodes - 1 - k) * inv + elim * bot
        hold_ref[k] = top
        hold_ref[nodes - 1 - k] = bot
        yield
    left = get(half - 1) + coef * top
    right = get(half) + coef * bot
    pivot = 1.0 + 2.0 * coef - coef * elim_ref[half - 2]
    even = (left + right) * (0.5 / (pivot - coef))
    odd = (left - right) * (0.5 / (pivot + coef))
    top, bot = even + odd, even - odd
    put(half - 1, top)
    put(half, bot)
    yield
    for k in range(half - 2, -1, -1):
        elim = elim_ref[k]
        top = hold_ref[k] + elim * top
        bot = hold_ref[nodes - 1 - k] + elim * bot
        put(k, top)
        put(nodes - 1 - k, bot)
        yield


def strided(rows_ref, lines, nodes):
    def get(n):
        return rows_ref[pl.ds(n, lines, stride=nodes + PAD), :]

    def put(n, value):
        rows_ref[pl.ds(n, lines, stride=nodes + PAD), :] = value

    return get, put


def dense(hold_ref):
    def get(n):
        return hold_ref[n]

    def put(n, value):
        hold_ref[n] = value

    return get, put


def run(steps, count=None):
    done = 0
    while count is None or done < count:
        if next(steps, steps) is steps:
            return
        done += 1


def pick(values, cross_hot):
    rows = values.shape[0]
    got = jnp.dot(jnp.concatenate(split3(values), axis=0), cross_hot, preferred_element_type=F32)
    return (got[:rows] + got[rows : 2 * rows]) + got[2 * rows :]


def place(values, cross_hot):
    rows = values.shape[0]
    got = dot_nt(jnp.concatenate(split3(values), axis=0), cross_hot)
    return (got[:rows] + got[rows : 2 * rows]) + got[2 * rows :]


def pack(leavers):
    rows = leavers.shape[0] // 2
    half = leavers.shape[1] // 2
    first, second = leavers[:rows], leavers[rows:]
    low = lax.broadcasted_iota(jnp.int32, first.shape, 1) < half
    up = jnp.where(low, first, pltpu.roll(second, half, 1))
    down = jnp.where(low, pltpu.roll(first, half, 1), second)
    return up, down


def unpack(up, down):
    half = up.shape[1] // 2
    low = lax.broadcasted_iota(jnp.int32, up.shape, 1) < half
    first = jnp.where(low, up, pltpu.roll(down, half, 1))
    second = jnp.where(low, pltpu.roll(up, half, 1), down)
    return first, second


def first_kernel(
    state_ref, index_ref, fill_ref, out_ref,
    table_ref, list_ref, held_ref, index_held_ref, fill_held_ref, sems, *, nodes, fdev
):
    pairs = (
        (fill_ref, fill_held_ref),
        (state_ref.at[pl.ds(0, 3 * nodes)], held_ref),
        (index_ref.at[0], index_held_ref),
    )
    copies = [pltpu.make_async_copy(src, dst, sems.at[i]) for i, (src, dst) in enumerate(pairs)]
    for copy in copies:
        copy.start()
    copies[0].wait()
    count = send_start(fill_held_ref, out_ref, list_ref, 0)
    copies[1].wait()
    store_table(table_ref, held_ref[...], nodes)
    copies[2].wait()
    send_gather(table_ref, index_held_ref, out_ref, list_ref, count, nodes, fdev)


def local_kernel(
    state_ref, coef_ref, cross_ref, index_ref,
    local_ref, inv_ref, elim_ref, rot_ref, up_ref, down_ref,
    table_ref, rows_ref, hold_ref, *, nodes, fdev,
):
    half_rows = 3 * nodes
    groups, lines, _ = local_ref.shape
    blocks = lines // 3
    coef = coef_ref[...]
    folded = fold_coef(coef, 3)
    fold(state_ref[half_rows:], rows_ref, nodes)
    store_table(table_ref, state_ref[:half_rows], nodes)

    def chores():
        yield from factor_steps(folded, inv_ref, elim_ref)
        sparse, close = strided(rows_ref, folded.shape[0], nodes), dense(hold_ref)
        for step in range(STEPS):
            get = sparse[0] if step == 0 else close[0]
            put = sparse[1] if step == STEPS - 1 else close[1]
            yield from solve_steps(get, put, hold_ref, folded, inv_ref, elim_ref, nodes)

    steps = chores()
    chunks = groups * blocks // CHUNK
    share = -(-(nodes // 2 + STEPS * nodes) // chunks)
    for i in range(chunks):
        ids = [i * CHUNK + k for k in range(CHUNK)]
        index = index_chunk(index_ref.at[0], ids, groups, blocks)
        rows = gather_row(table_ref[...], index, nodes, fdev, lambda: run(steps, share))
        put_chunk(local_ref, ids, rows, blocks)
    run(steps)

    rot_ref[...] = unfold(rows_ref, half_rows, nodes)
    cross_hot = hot(cross_ref[pl.ds(0, 1), :], fdev)
    leave(rot_ref[...], coef, cross_hot, up_ref, down_ref)


def leave(rot, coef, cross_hot, up_ref, down_ref):
    up, down = pack(pick(rot, cross_hot))
    rows = up.shape[0]
    up_ref[:rows] = up
    down_ref[:rows] = down
    moved = pick(jnp.broadcast_to(coef, (8, coef.shape[1])), cross_hot)
    up_ref[rows:] = moved
    down_ref[rows:] = pltpu.roll(moved, moved.shape[1] // 2, 1)


def local_next_kernel(
    up_ref, down_ref, pos_ref, rot_ref, coef_ref, cross_ref, index_ref, told_ref,
    state_ref, local_ref, inv_ref, elim_ref, rot_out_ref, coef_out_ref, rup_ref, rdown_ref,
    table_ref, list_ref, *, step, nodes, fdev,
):
    groups, lines, _ = local_ref.shape
    blocks = lines // 3
    part = 3 * nodes // 2
    words = live_words(told_ref, blocks, BLOCK // 2)
    count = list_live(lambda g, b: (words[g] >> b) & 1, list_ref, groups, blocks)
    local_ref[...] = jnp.zeros_like(local_ref)
    cross_hot = hot(cross_ref[pl.ds(step - 1, 1), :], fdev)
    keep = kept(cross_hot)
    rows = pl.ds(3 * nodes, 8)
    first, _ = unpack(up_ref[rows, :], down_ref[rows, :])
    coef = jnp.where(keep, coef_ref[...], place(first, cross_hot)[0:1])
    coef_out_ref[...] = coef
    positions = arrive(up_ref, down_ref, pos_ref[...], cross_hot, keep, 0)
    state_ref[...] = positions
    store_table(table_ref, positions, nodes)
    run(factor_steps(fold_coef(coef, 3), inv_ref, elim_ref))
    rot = arrive(up_ref, down_ref, rot_ref[...], cross_hot, keep, part)
    rot_out_ref[...] = rot
    leave(rot, coef, hot(cross_ref[pl.ds(step, 1), :], fdev), rup_ref, rdown_ref)
    gather_live(
        index_ref.at[step], local_ref, list_ref, count, groups, blocks,
        lambda index: gather_row(table_ref[...], index, nodes, fdev),
    )


def contact_kernel(
    got_ref, local_ref, index_ref, state_ref, coef_ref, inv_ref, elim_ref, cross_ref, rup_ref, rdown_ref,
    pos_ref, up_ref, down_ref,
    acc_ref, rows_ref, hold_ref, force_ref, list_ref, *, step, nodes, fdev,
):
    half_rows = 3 * nodes
    groups, lines, _ = local_ref.shape
    blocks = lines // 3
    pairs = groups * blocks
    acc_ref[...] = jnp.zeros_like(acc_ref)
    force_ref[:, pairs:] = jnp.zeros_like(force_ref[:, pairs:])
    lanes = lax.broadcasted_iota(jnp.int32, (blocks, BLOCK), 1).astype(F32)
    words = live_words(got_ref, blocks, 0)
    for g in range(groups):
        delta = [
            got_ref[g, c * blocks : (c + 1) * blocks] - local_ref[g, c * blocks : (c + 1) * blocks] for c in range(3)
        ]
        radius = delta[0] * delta[0] + delta[1] * delta[1] + delta[2] * delta[2]
        live = lanes < got_ref[g, 3 * blocks :, 0:1]
        scale = 1.0 / (1.0 + radius)
        for c in range(3):
            force_ref[c, g * blocks : (g + 1) * blocks] = jnp.where(live, delta[c] * scale, 0.0)
    count = list_live(lambda g, b: (words[g] >> b) & 1, list_ref, groups, blocks)
    wide = fdev // LANES
    keys = wide * nodes

    def body(numbers):
        places = [i * CHUNK + k for i in numbers for k in range(CHUNK)]
        ids = [jnp.where(n < count, list_ref[n], pairs) for n in places]
        index = index_chunk(index_ref.at[step], [jnp.minimum(n, pairs - 1) for n in ids], groups, blocks)
        lane, per_node = parts_of(index, nodes)
        key = row_key(per_node, nodes, fdev)
        mask = lax.broadcasted_iota(jnp.int32, (keys, index.shape[1]), 0) == key
        highs, lows = [], []
        for c in range(3):
            force = jnp.concatenate([force_ref[c, pl.ds(n, 1), :] for n in ids], axis=1)
            hi, lo = split2(force)
            highs.append(jnp.where(mask, hi.astype(F32), 0.0).astype(BF16))
            lows.append(jnp.where(mask, lo.astype(F32), 0.0).astype(BF16))
        spread = jnp.concatenate(highs + lows, axis=0)
        acc_ref[...] += dot_nt(spread, hot(lane, LANES))

    each_chunk(count, body)

    total = acc_ref[: 3 * keys] + acc_ref[3 * keys :]
    contact = jnp.concatenate(
        [
            jnp.concatenate([total[(c * wide + w) * nodes : (c * wide + w + 1) * nodes] for c in range(3)], axis=0)
            for w in range(wide)
        ],
        axis=1,
    )
    fold(state_ref[:half_rows] + 0.5 * contact, rows_ref, nodes)
    folded = fold_coef(coef_ref[...], 3)
    get, put = strided(rows_ref, folded.shape[0], nodes)
    run(solve_steps(get, put, hold_ref, folded, inv_ref, elim_ref, nodes))
    pos_ref[...] = unfold(rows_ref, half_rows, nodes)
    up, down = pack(pick(pos_ref[...], hot(cross_ref[pl.ds(step, 1), :], fdev)))
    rows = up.shape[0]
    up_ref[:rows] = up
    down_ref[:rows] = down
    up_ref[rows:] = rup_ref[...]
    down_ref[rows:] = rdown_ref[...]


def kept(cross_hot):
    ones = jnp.ones((8, cross_hot.shape[1]), BF16)
    return dot_nt(ones, cross_hot)[0:1] < 0.5


def arrive(up_ref, down_ref, values, cross_hot, keep, at):
    rows = pl.ds(at, values.shape[0] // 2)
    first, second = unpack(up_ref[rows, :], down_ref[rows, :])
    return jnp.where(keep, values, place(jnp.concatenate([first, second], axis=0), cross_hot))


def own_kernel(
    pos_ref, cross_ref, index_ref, fill_ref, out_ref, table_ref, list_ref, fill_held_ref, sem, *, step, nodes, fdev
):
    copy = pltpu.make_async_copy(fill_ref, fill_held_ref, sem)
    copy.start()
    keep = kept(hot(cross_ref[pl.ds(step - 1, 1), :], fdev))
    store_table(table_ref, jnp.where(keep, pos_ref[...], 0.0), nodes)
    copy.wait()
    count = send_start(fill_held_ref, out_ref, list_ref, step)
    send_gather(table_ref, index_ref.at[step], out_ref, list_ref, count, nodes, fdev)


def next_kernel(
    up_ref, down_ref, own_ref, cross_ref, index_ref, out_ref, table_ref, list_ref, *, step, nodes, fdev
):
    groups, lines, _ = out_ref.shape
    blocks = lines // 4
    words = live_words(own_ref, blocks, 0)
    count = list_live(lambda g, b: (words[g] >> b) & 1, list_ref, groups, blocks)
    out_ref[...] = own_ref[...]
    cross = cross_ref[pl.ds(step - 1, 1), :]
    moved = cross.shape[1]
    here = lax.broadcasted_iota(jnp.int32, (moved, moved), 0) == lax.broadcasted_iota(jnp.int32, (moved, moved), 1)
    slots = jnp.sum(jnp.where(here, cross.astype(F32), 0.0), axis=1, keepdims=True).astype(jnp.int32)
    part = 3 * nodes // 2
    first, second = unpack(up_ref[:part, :], down_ref[:part, :])
    hi, lo = split2(jnp.concatenate([first, second], axis=0))
    table_ref[: 2 * part] = hi
    table_ref[2 * part :] = lo

    def body(numbers):
        for i in numbers:
            ids = [list_ref[jnp.minimum(i * CHUNK + k, count - 1)] for k in range(CHUNK)]
            rows = arrived_row(table_ref[...], slots, index_chunk(index_ref.at[step], ids, groups, blocks), fdev)
            held = get_chunk(own_ref, ids, blocks)
            put_chunk(out_ref, ids, [a + b for a, b in zip(held, rows)], blocks)

    each_chunk(count, body)


def last_kernel(up_ref, down_ref, pos_ref, rot_ref, cross_ref, state_ref, done_ref, sems, *, step, nodes, fdev):
    rows = 3 * nodes
    cross_hot = hot(cross_ref[pl.ds(step, 1), :], fdev)
    keep = kept(cross_hot)
    copies = []
    for i, ref in enumerate((pos_ref, rot_ref)):
        side = pl.ds(i * rows, rows)
        done_ref[side, :] = arrive(up_ref, down_ref, ref[...], cross_hot, keep, i * rows // 2)
        copies.append(pltpu.make_async_copy(done_ref.at[side], state_ref.at[side], sems.at[i]))
        copies[i].start()
    for copy in copies:
        copy.wait()


def shifted(block, axis, distance):
    devices = range(lax.axis_size(axis))
    route = [((i - distance) % len(devices), i) for i in devices]
    return lax.ppermute(block, axis, route)


def per_device(state, stiffness, crossing, contact_send, contact_recv, contact_fill):
    fields, nodes, fdev = state.shape
    _, groups, quota = contact_send.shape
    blocks = quota // BLOCK
    pairs = groups * blocks
    cross = crossing.shape[1]
    rows = 3 * nodes
    moved = rows + 8
    lines = 3 * fdev // BLOCK
    vmem = pl.BlockSpec(memory_space=pltpu.VMEM)
    hbm = pl.BlockSpec(memory_space=pltpu.HBM)
    table = pltpu.VMEM((2 * rows * fdev // LANES, LANES), BF16)
    listed = pltpu.SMEM((pairs + 1,), jnp.int32)
    folded = pltpu.VMEM((lines * (nodes + PAD), BLOCK), F32)

    def sds(*shape):
        return jax.ShapeDtypeStruct(shape, F32)

    sent_shape = sds(groups, 4 * blocks, BLOCK)
    factors = sds(nodes // 2, lines, BLOCK)

    fills = pltpu.SMEM(contact_fill.shape, jnp.int32)
    hold = pltpu.VMEM((nodes, lines, BLOCK), F32)

    def call(kernel, name, ins, outs, scratch, flops, limit=VMEM_LIMIT, space=vmem, **static):
        return pl.pallas_call(
            functools.partial(kernel, nodes=nodes, fdev=fdev, **static),
            out_shape=outs,
            in_specs=ins,
            out_specs=[space] * len(outs),
            scratch_shapes=scratch,
            name=name,
            cost_estimate=pl.CostEstimate(flops=flops, bytes_accessed=4 * fields * nodes * fdev, transcendentals=0),
            compiler_params=pltpu.CompilerParams(vmem_limit_bytes=limit),
        )

    def by_block(index):
        return index.reshape(-1, groups, blocks, BLOCK).transpose(0, 2, 1, 3).reshape(-1, pairs, BLOCK)

    send, recv = by_block(contact_send), by_block(contact_recv)
    matmul = 2 * 2 * rows * fdev * groups * quota
    xcur = state.reshape(fields * nodes, fdev)
    coef = stiffness.reshape(1, fdev)
    (sent,) = call(
        first_kernel, "send_first", [hbm] * 3, [sent_shape],
        [table, listed, pltpu.VMEM((rows, fdev), F32), pltpu.VMEM((pairs, BLOCK), jnp.int32),
         fills, pltpu.SemaphoreType.DMA((3,))], matmul, limit=FIRST_LIMIT,
    )(xcur, send, contact_fill)
    got_shape = sds(groups, 3 * blocks, BLOCK)
    rot_moved = sds(rows // 2 + 8, cross)
    for step in range(STEPS):
        told = None if step == 0 else got
        got = lax.all_to_all(sent, "span", split_axis=0, concat_axis=0, tiled=True)
        if step == 0:
            local, inv, elim, rot, rup, rdown = call(
                local_kernel, "local", [vmem] * 4,
                [got_shape, factors, factors, sds(rows, fdev), rot_moved, rot_moved],
                [table, folded, hold], matmul,
            )(xcur, coef, crossing, recv)
        else:
            xcur, local, inv, elim, rot, coef, rup, rdown = call(
                local_next_kernel, "local_next", [vmem] * 8,
                [sds(rows, fdev), got_shape, factors, factors, sds(rows, fdev), sds(1, fdev), rot_moved, rot_moved],
                [table, listed], matmul, step=step,
            )(up, down, pos, rot, coef, crossing, recv, told)
        pos, up, down = call(
            contact_kernel, "contact", [vmem] * 10,
            [sds(rows, fdev), sds(moved, cross), sds(moved, cross)],
            [pltpu.VMEM((2 * rows * fdev // LANES, LANES), F32), folded, hold,
             pltpu.VMEM((3, pairs + 8, BLOCK), F32), listed], matmul, step=step,
        )(got, local, recv, xcur, coef, inv, elim, crossing, rup, rdown)
        up = shifted(up, "stream", 1)
        down = shifted(down, "stream", -1)
        if step + 1 < STEPS:
            (own,) = call(
                own_kernel, "send_own", [vmem] * 4, [sent_shape],
                [table, listed, fills, pltpu.SemaphoreType.DMA(())], matmul, step=step + 1,
            )(pos, crossing, send, contact_fill)
            (sent,) = call(
                next_kernel, "send_next", [vmem] * 5, [sent_shape],
                [pltpu.VMEM((2 * rows, cross), BF16), listed], matmul, step=step + 1,
            )(up, down, own, crossing, send)
        else:
            (xcur,) = call(
                last_kernel, "arrive", [vmem] * 5, [sds(fields * nodes, fdev)],
                [pltpu.VMEM((fields * nodes, fdev), F32), pltpu.SemaphoreType.DMA((2,))],
                matmul // 8, space=hbm, step=step,
            )(up, down, pos, rot, crossing)
    return xcur.reshape(fields, nodes, fdev)


def solution(mesh):
    placed = (
        P(None, None, ("span", "stream")),
        P(("span", "stream")),
        P(None, ("span", "stream")),
        P(None, None, ("span", "stream")),
        P(None, None, ("span", "stream")),
        P(None, None, ("span", "stream")),
    )
    return jax.shard_map(
        per_device,
        mesh=mesh,
        in_specs=placed,
        out_specs=P(None, None, ("span", "stream")),
        check_vma=False,
    )
```
